128 devices in a mesh: pipe: 2 (over x_lo), dp: 64 (over z, x_hi, y, core).
Axes of the slice: x: 4 (x_hi: 2, x_lo: 2; x = x_hi * 2 + x_lo), y: 4, z: 4, core: 2. Of those that a mesh axis runs over, the one named last changes fastest.
Arguments:
- segment_input: bfloat16 [2, 512, 12288], P('pipe', 'dp'), may hold values from -3000 to 3000, as said below
- norm_gain: float32 [2, 12288], P('pipe'), may hold values from 0.5 to 2
- head_weights: bfloat16 [2, 12288, 64, 384], P('pipe', None, 'dp'), may hold values from -0.04818163 to 0.04818163
- output_weights: bfloat16 [2, 8192, 12288], P('pipe', 'dp'), may hold values from -0.25 to 0.25
Outputs:
- section_outputs: bfloat16 [2, 512, 12288], P('pipe', 'dp')
The draws below stay inside these ranges and needn't reach their ends.
Inputs may be any that keep to these rules, and one draw needn't show every extreme that they name: `segment_input`: activations of order one to some thousands, rows and features of unlike scales.
All inputs are finite; a program needn't handle non-finite values.
Results may differ from the reference program's by a relative error of at most 0.0083.
Values may be sent and summed in bfloat16 or wider, within the bound.
No kernel may reach another device: no remote copies, remote signals or barrier semaphores. Data moves between devices by JAX's collectives and lax.ppermute only.
A program may use at most 128 MiB of HBM per device.

```python
import math
import jax
import jax.numpy as jnp
from jax import lax

D = 12288
HEAD_DIM = 128
HEADS = 64
TOKENS = 512
N_PIPE = 2


def draw_segment_input(key, part):
    column_scale = jnp.exp(jax.random.uniform(jax.random.fold_in(key, 21), (N_PIPE, 1, D), jnp.float32) * math.log(10.0))
    row_scale = jnp.exp(jax.random.uniform(jax.random.fold_in(key, 22), (N_PIPE, TOKENS, 1), jnp.float32) * math.log(10.0))
    base = jax.random.truncated_normal(jax.random.fold_in(key, 26), -6.0, 6.0, (N_PIPE, TOKENS, D), jnp.float32)
    result = row_scale * column_scale * base
    return result.astype(jnp.bfloat16)


def draw_head_weights(key, part):
    base = jax.random.truncated_normal(jax.random.fold_in(key, 30), -4.0, 4.0, (N_PIPE, D, HEADS, 3 * HEAD_DIM), jnp.float32) / math.sqrt(D)
    return base.astype(jnp.bfloat16)


def block_levels(rng, shape, split, least, high):
    loudness, own = 1.0, jax.random.fold_in(rng, 6)
    for dim, shards_of in split:
        steps = jnp.exp(jax.random.uniform(jax.random.fold_in(own, dim), (shards_of,), jnp.float32, least / len(split), high / len(split)))
        loudness = loudness * jnp.repeat(steps, shape[dim] // shards_of).reshape([-1 if axis == dim else 1 for axis in range(len(shape))])
    return loudness


def gaussian(rng, dims, scale, bound, cuts=(), kind=jnp.bfloat16):
    drawn = scale * jax.random.normal(rng, dims, jnp.float32)
    if cuts:
        drawn = drawn * block_levels(rng, dims, cuts, -0.22, 0.18)
    return jnp.clip(drawn, -bound, bound).astype(kind)


def setup_inputs(seed: int = 0) -> dict:
    key_of = jax.random.split(jax.random.key(seed), 5)
    segment_input = draw_segment_input(jax.random.fold_in(key_of[4], 71), 0)
    norm_gain = jnp.clip(jnp.exp(math.log(2.0) - 1.3862944 * jax.random.uniform(key_of[1], (N_PIPE, D), jnp.float32) ** block_levels(key_of[1], (N_PIPE, D), ((0, 2),), -0.2, 0.2)), 0.5, 2.0)
    head_weights = draw_head_weights(jax.random.fold_in(key_of[4], 71), 0)
    output_weights = gaussian(key_of[3], (N_PIPE, HEADS * HEAD_DIM, D), (4 * HEAD_DIM) ** -0.5, 0.25, ((0, 2), (1, 64)))
    return {"segment_input": segment_input, "norm_gain": norm_gain, "head_weights": head_weights, "output_weights": output_weights}


def normalize(section_rows, gain_vector):
    values = section_rows.astype(jnp.float32)
    centre = lax.optimization_barrier(jnp.mean(values, axis=-1, keepdims=True))
    shifted = values - centre
    spread = lax.optimization_barrier(jnp.mean(shifted * shifted, axis=-1, keepdims=True))
    return (shifted * lax.rsqrt(spread + 1e-05) * gain_vector).astype(jnp.bfloat16)

def attend(projected, head_size):
    queries = projected[:, :head_size]
    keys_part = projected[:, head_size:2 * head_size]
    values_part = projected[:, 2 * head_size:].astype(jnp.bfloat16)
    scores = jnp.einsum('qd,kd->qk', queries, keys_part, precision=lax.Precision.HIGHEST) / math.sqrt(head_size)
    length = projected.shape[0]
    causal = jnp.arange(length)[:, None] >= jnp.arange(length)[None, :]
    scores = jnp.where(causal, scores, -1e+30)
    largest = lax.optimization_barrier(jnp.max(scores, axis=-1, keepdims=True))
    weights = jnp.where(causal, jnp.exp(scores - largest), 0.0)
    totals = lax.optimization_barrier(jnp.sum(weights, axis=-1, keepdims=True))
    probabilities = (weights / totals).astype(jnp.bfloat16)
    return jnp.dot(probabilities, values_part, preferred_element_type=jnp.float32).astype(jnp.bfloat16)

def section(section_rows, gain_vector, weights_block, output_block):
    normed = normalize(section_rows, gain_vector)

    def add_head(head_index, running):
        index_now = jnp.asarray(head_index).astype(jnp.int32)
        head_block = lax.dynamic_index_in_dim(weights_block, index_now, axis=1, keepdims=False)
        projected = jnp.dot(normed, head_block, preferred_element_type=jnp.float32)
        attended = attend(projected, HEAD_DIM)
        out_start = (index_now * HEAD_DIM).astype(jnp.int32)
        out_rows = lax.dynamic_slice_in_dim(output_block, out_start, HEAD_DIM, 0)
        return running + jnp.dot(attended, out_rows, preferred_element_type=jnp.float32)
    initial = jnp.zeros((section_rows.shape[0], D), jnp.float32)
    summed = lax.fori_loop(0, HEADS, add_head, initial)
    return summed.astype(jnp.bfloat16)

def reference(segment_input, norm_gain, head_weights, output_weights):
    second = section(segment_input[1], norm_gain[1], head_weights[1], output_weights[1])
    first = section(segment_input[0], norm_gain[0], head_weights[0], output_weights[0])
    return jnp.stack([second, first])
```

```python
import math

import jax
import jax.numpy as jnp
import numpy as np
from jax import lax
from jax.sharding import PartitionSpec as P

RING = 4
AXES = ("pipe", "dp")


def split_place(index):
    core = index % 2
    y = index // 2 % 4
    half_x = index // 8 % 2
    z = index // 16 % 4
    pipe = index // 64
    return pipe, z, half_x, y, core


def join_place(pipe, z, half_x, y, core):
    return (((pipe * 4 + z) * 2 + half_x) * 4 + y) * 2 + core


def send(value, pipe=0, z=0, x=0, y=0, core=0):
    pairs = []
    for source in range(128):
        p0, z0, x0, y0, c0 = split_place(source)
        target = join_place(p0 ^ pipe, (z0 + z) % 4, x0 ^ x, (y0 + y) % 4, c0 ^ core)
        pairs.append((source, target))
    return lax.ppermute(value, AXES, pairs)


def normalize(section_rows, gain_vector):
    values = section_rows.astype(jnp.float32)
    centre = jnp.mean(values, axis=-1, keepdims=True)
    shifted = values - centre
    spread = jnp.mean(shifted * shifted, axis=-1, keepdims=True)
    return (shifted * lax.rsqrt(spread + 1e-05) * gain_vector).astype(jnp.bfloat16)


def ring_gather(block, axis):
    half = block.shape[0] // 2
    top, bottom = block[:half], block[half:]
    top_before = send(top, **{axis: 1})
    bottom_after = send(bottom, **{axis: -1})
    bottom_before = send(bottom, **{axis: 1})
    top_after = send(top, **{axis: -1})
    top_far = send(top_before, **{axis: 1})
    bottom_far = send(bottom_after, **{axis: -1})
    return (
        (top, bottom),
        (top_after, bottom_after),
        (top_before, bottom_before),
        (top_far, bottom_far),
    )


def rows_of(*pairs):
    return jnp.concatenate([piece for pair in pairs for piece in pair], axis=0)


def ring_scatter(far, after, before, own, axis):
    half = far.shape[0] // 2
    from_before = send(far[:half], **{axis: 1})
    from_after = send(far[half:], **{axis: -1})
    to_after = jnp.concatenate(
        [after[:half] + from_before.astype(jnp.float32), after[half:]], axis=0
    ).astype(jnp.bfloat16)
    to_before = jnp.concatenate(
        [before[:half], before[half:] + from_after.astype(jnp.float32)], axis=0
    ).astype(jnp.bfloat16)
    got_before = send(to_after, **{axis: 1})
    got_after = send(to_before, **{axis: -1})
    return own + got_before.astype(jnp.float32) + got_after.astype(jnp.float32)


def small_scatter(chunks, axis):
    size = chunks.shape[0] // 4
    parts = [chunks[k * size : (k + 1) * size] for k in range(4)]
    total = parts[0]
    for part, step in ((parts[1], 1), (parts[2], -1), (parts[3], 2)):
        total = total + send(part.astype(jnp.bfloat16), **{axis: step}).astype(jnp.float32)
    return total


def token_positions(z, y):
    steps = (0, 1, -1, 2)
    dz, dy, xs, low = [], [], [], []
    for side, far_step in (
        (0, 2), (1, 2), (0, 1), (0, -1), (1, 1), (1, -1), (0, 0), (1, 0),
    ):
        for near in steps:
            for r in range(16):
                dz.append(far_step if side == 0 else near)
                dy.append(near if side == 0 else far_step)
                xs.append(side)
                low.append(r)
    dz, dy, xs, low = (np.asarray(v, np.int32) for v in (dz, dy, xs, low))
    return ((((z + dz) % 4) * 2 + xs) * 4 + (y + dy) % 4) * 16 + low


def attend(projected, position, head_size):
    queries = projected[:, :head_size]
    keys_part = projected[:, head_size : 2 * head_size]
    values_part = projected[:, 2 * head_size :].astype(jnp.bfloat16)
    scores = jnp.einsum(
        "qd,kd->qk", queries, keys_part, precision=lax.Precision.HIGHEST
    ) / math.sqrt(head_size)
    causal = position[:, None] >= position[None, :]
    scores = jnp.where(causal, scores, -1e30)
    largest = jnp.max(scores, axis=-1, keepdims=True)
    weights = jnp.where(causal, jnp.exp(scores - largest), 0.0)
    totals = jnp.sum(weights, axis=-1, keepdims=True)
    probabilities = (weights / totals).astype(jnp.bfloat16)
    return jnp.dot(probabilities, values_part, preferred_element_type=jnp.float32).astype(
        jnp.bfloat16
    )


def shards(segment_input, norm_gain, head_weights, output_weights):
    head_size = output_weights.shape[1]
    width = segment_input.shape[2]
    half, quarter = width // 2, width // 4
    _, z, half_x, y, core = split_place(lax.axis_index("dp"))

    normed = normalize(segment_input[0], norm_gain[0])
    left, right = normed[:, :half], normed[:, half:]
    kept = jnp.where(core == 0, left, right)
    given = send(jnp.where(core == 0, right, left), core=1)
    block = jnp.where(
        core == 0, jnp.concatenate([kept, given]), jnp.concatenate([given, kept])
    )
    other = send(block, x=1)
    first = jnp.where(half_x == 0, block, other)
    second = jnp.where(half_x == 0, other, block)

    head_block = head_weights[0, :, 0, :]
    own_weights = lax.dynamic_slice_in_dim(head_block, core * half, half, 0)
    swapped_weights = send(
        lax.dynamic_slice_in_dim(head_block, (1 - core) * half, half, 0), core=1
    )
    out_rows = output_weights[0]
    out_parts = []
    for dx, dc in ((0, 0), (0, 1), (1, 0), (1, 1)):
        start = ((half_x ^ dx) * 2 + (core ^ dc)) * quarter
        part = lax.dynamic_slice_in_dim(out_rows, start, quarter, 1)
        out_parts.append(send(part, x=dx, core=dc) if dx or dc else part)
    out_block = jnp.concatenate(out_parts, axis=0)

    first_near = rows_of(*ring_gather(first, "y"))
    second_near = rows_of(*ring_gather(second, "z"))
    first_all = ring_gather(first_near, "z")
    second_all = ring_gather(second_near, "y")

    def project(rows):
        mine = jnp.dot(rows, own_weights, preferred_element_type=jnp.float32)
        theirs = jnp.dot(rows, swapped_weights, preferred_element_type=jnp.float32)
        return mine + send(theirs, core=1)

    near = project(jnp.concatenate([first_near, second_near]))
    middle = project(
        rows_of(first_all[1], first_all[2], second_all[1], second_all[2])
    )
    far = project(rows_of(first_all[3], second_all[3]))
    projected = jnp.concatenate([far, middle, near], axis=0)

    attended = attend(projected, token_positions(z, y), head_size)
    across_x = send(attended, x=1)
    across_core = send(attended, core=1)
    across_both = send(across_x, core=1)
    heads = jnp.concatenate([attended, across_core, across_x, across_both], axis=1)

    edge = jnp.dot(heads[:128], out_block, preferred_element_type=jnp.float32).astype(
        jnp.bfloat16
    )
    rest = jnp.dot(heads[128:], out_block, preferred_element_type=jnp.float32)
    first_sum = ring_scatter(
        edge[:64], rest[:64], rest[64:128], rest[256:320], "z"
    )
    second_sum = ring_scatter(
        edge[64:], rest[128:192], rest[192:256], rest[320:384], "y"
    )
    first_rows = small_scatter(first_sum, "y").astype(jnp.bfloat16)
    second_rows = small_scatter(second_sum, "z").astype(jnp.bfloat16)

    owners = jnp.stack([first_rows, second_rows]).reshape(2, 2, 8, quarter)
    by_x = jnp.where(half_x == 0, owners, owners[::-1])
    by_place = jnp.where(core == 0, by_x, by_x[:, ::-1])
    got = jnp.stack(
        [
            jnp.stack([send(by_place[dx, dc], pipe=1, x=dx, core=dc) for dc in (0, 1)])
            for dx in (0, 1)
        ]
    )
    got = jnp.where(core == 0, got, got[:, ::-1])
    got = jnp.where(half_x == 0, got, got[::-1])
    return jnp.concatenate([got[0, 0], got[0, 1], got[1, 0], got[1, 1]], axis=1)[None]


def solution(mesh):
    placed = (
        P("pipe", "dp", None),
        P("pipe", None),
        P("pipe", None, "dp", None),
        P("pipe", "dp", None),
    )
    return jax.shard_map(
        shards, mesh=mesh, in_specs=placed, out_specs=P("pipe", "dp", None), check_vma=False
    )
```

```python
import math

import jax
import jax.numpy as jnp
import numpy as np
from jax import lax
from jax.sharding import PartitionSpec as P

RING = 4
AXES = ("pipe", "dp")


def split_place(index):
    core = index % 2
    y = index // 2 % 4
    half_x = index // 8 % 2
    z = index // 16 % 4
    pipe = index // 64
    return pipe, z, half_x, y, core


def join_place(pipe, z, half_x, y, core):
    return (((pipe * 4 + z) * 2 + half_x) * 4 + y) * 2 + core


def send(value, pipe=0, z=0, x=0, y=0, core=0):
    pairs = []
    for source in range(128):
        p0, z0, x0, y0, c0 = split_place(source)
        target = join_place(p0 ^ pipe, (z0 + z) % 4, x0 ^ x, (y0 + y) % 4, c0 ^ core)
        pairs.append((source, target))
    return lax.ppermute(value, AXES, pairs)


def normalize(section_rows, gain_vector):
    values = section_rows.astype(jnp.float32)
    centre = jnp.mean(values, axis=-1, keepdims=True)
    shifted = values - centre
    spread = jnp.mean(shifted * shifted, axis=-1, keepdims=True)
    return (shifted * lax.rsqrt(spread + 1e-05) * gain_vector).astype(jnp.bfloat16)


def onward(value, axis):
    pairs = []
    for source in range(128):
        pipe, z, half_x, y, core = split_place(source)
        step = 1 - 2 * core
        if axis == "z":
            z = (z + step) % RING
        else:
            y = (y + step) % RING
        pairs.append((source, join_place(pipe, z, half_x, y, core)))
    return lax.ppermute(value, AXES, pairs)


def both_onward(first, first_axis, second, second_axis, *beside):
    first, second = lax.optimization_barrier((first, second))
    first, second = onward(first, first_axis), onward(second, second_axis)
    return lax.optimization_barrier((first, second, *beside))


def both_scatter(first, first_axis, second, second_axis):
    narrow = jnp.bfloat16
    first_sum, second_sum = first[1].astype(narrow), second[1].astype(narrow)
    for k in (2, 3, 0):
        first_got, second_got = both_onward(
            first_sum, first_axis, second_sum, second_axis
        )
        first_sum = first[k] + first_got.astype(jnp.float32)
        second_sum = second[k] + second_got.astype(jnp.float32)
        if k:
            first_sum, second_sum = first_sum.astype(narrow), second_sum.astype(narrow)
    return first_sum, second_sum


def mirrored(value):
    blocks = value.reshape(4, 2, 4, 16, value.shape[1])
    blocks = jnp.stack([blocks[2], blocks[1], blocks[0], blocks[3]])
    blocks = jnp.stack(
        [blocks[:, :, 0], blocks[:, :, 3], blocks[:, :, 2], blocks[:, :, 1]], axis=2
    )
    return blocks.reshape(value.shape)


def token_positions(z, y, core):
    far = np.repeat(np.asarray([1, 2, 3, 0], np.int32), 128)
    side = np.tile(np.repeat(np.asarray([0, 1], np.int32), 64), 4)
    near = np.tile(np.repeat(np.arange(4, dtype=np.int32), 16), 8)
    low = np.tile(np.arange(16, dtype=np.int32), 32)
    step = 1 - 2 * core
    dz = np.where(side == 0, far, near)
    dy = np.where(side == 0, near, far)
    return (((z - step * dz) % 4 * 2 + side) * 4 + (y - step * dy) % 4) * 16 + low


def attend(projected, position, head_size):
    queries = projected[:, :head_size]
    keys_part = projected[:, head_size : 2 * head_size]
    values_part = projected[:, 2 * head_size :].astype(jnp.bfloat16)
    scores = jnp.einsum(
        "qd,kd->qk", queries, keys_part, precision=lax.Precision.HIGHEST
    ) / math.sqrt(head_size)
    causal = position[:, None] >= position[None, :]
    scores = jnp.where(causal, scores, -1e30)
    largest = jnp.max(scores, axis=-1, keepdims=True)
    weights = jnp.where(causal, jnp.exp(scores - largest), 0.0)
    totals = jnp.sum(weights, axis=-1, keepdims=True)
    probabilities = (weights / totals).astype(jnp.bfloat16)
    return jnp.dot(probabilities, values_part, preferred_element_type=jnp.float32).astype(
        jnp.bfloat16
    )


def shards(segment_input, norm_gain, head_weights, output_weights):
    head_size = output_weights.shape[1]
    width = segment_input.shape[2]
    half, quarter = width // 2, width // 4
    _, z, half_x, y, core = split_place(lax.axis_index("dp"))

    normed = normalize(segment_input[0], norm_gain[0])
    left, right = normed[:, :half], normed[:, half:]
    kept = jnp.where(core == 0, left, right)
    given = send(jnp.where(core == 0, right, left), core=1)
    block = jnp.where(
        core == 0, jnp.concatenate([kept, given]), jnp.concatenate([given, kept])
    )
    head_block, out_rows, block = lax.optimization_barrier(
        (head_weights[0, :, 0, :], output_weights[0], block)
    )
    other = send(block, x=1)
    first = jnp.where(half_x == 0, block, other)
    second = jnp.where(half_x == 0, other, block)
    own_weights = lax.dynamic_slice_in_dim(head_block, core * half, half, 0)
    swapped_weights = send(
        lax.dynamic_slice_in_dim(head_block, (1 - core) * half, half, 0), core=1
    )
    out_parts = []
    for dx, dc in ((0, 0), (0, 1), (1, 0), (1, 1)):
        start = ((half_x ^ dx) * 2 + (core ^ dc)) * quarter
        part = lax.dynamic_slice_in_dim(out_rows, start, quarter, 1)
        out_parts.append(send(part, x=dx, core=dc) if dx or dc else part)
    out_block = jnp.concatenate(out_parts, axis=0)

    first_near, second_near = [first], [second]
    for _ in range(3):
        got = both_onward(first_near[-1], "y", second_near[-1], "z")
        first_near.append(got[0])
        second_near.append(got[1])
    first_far = [jnp.concatenate(first_near)]
    second_far = [jnp.concatenate(second_near)]

    def project(rows):
        mine = jnp.dot(rows, own_weights, preferred_element_type=jnp.float32)
        theirs = jnp.dot(rows, swapped_weights, preferred_element_type=jnp.float32)
        return mine, theirs

    mine, theirs = [], []
    for k in range(4):
        here = project(jnp.concatenate([first_far[k], second_far[k]]))
        if k < 3:
            got = both_onward(first_far[k], "z", second_far[k], "y", *here)
            first_far.append(got[0])
            second_far.append(got[1])
            here = got[2:]
        mine.append(here[0])
        theirs.append(send(here[1], core=1))
    projected = []
    for k in (1, 2, 3, 0):
        back = theirs[-k % 4].reshape(2, 4, 16, -1)
        back = jnp.stack([back[:, 0], back[:, 3], back[:, 2], back[:, 1]], axis=1)
        projected.append(mine[k] + back.reshape(mine[k].shape))
    projected = jnp.concatenate(projected)

    attended = attend(projected, token_positions(z, y, core), head_size)
    across_x = send(attended, x=1)
    across_core = send(mirrored(attended), core=1)
    across_both = send(mirrored(across_x), core=1)
    heads = jnp.concatenate([attended, across_core, across_x, across_both], axis=1)

    edge = jnp.dot(heads[:128], out_block, preferred_element_type=jnp.float32)
    rest = jnp.dot(heads[128:], out_block, preferred_element_type=jnp.float32)
    first_sum, second_sum = both_scatter(
        (rest[256:320], edge[:64], rest[:64], rest[128:192]),
        "z",
        (rest[320:384], edge[64:], rest[64:128], rest[192:256]),
        "y",
    )
    first_rows, second_rows = both_scatter(
        first_sum.reshape(4, 16, quarter), "y", second_sum.reshape(4, 16, quarter), "z"
    )
    first_rows = first_rows.astype(jnp.bfloat16)
    second_rows = second_rows.astype(jnp.bfloat16)

    owners = jnp.stack([first_rows, second_rows]).reshape(2, 2, 8, quarter)
    by_x = jnp.where(half_x == 0, owners, owners[::-1])
    by_place = jnp.where(core == 0, by_x, by_x[:, ::-1])
    got = jnp.stack(
        [
            jnp.stack([send(by_place[dx, dc], pipe=1, x=dx, core=dc) for dc in (0, 1)])
            for dx in (0, 1)
        ]
    )
    got = jnp.where(core == 0, got, got[:, ::-1])
    got = jnp.where(half_x == 0, got, got[::-1])
    return jnp.concatenate([got[0, 0], got[0, 1], got[1, 0], got[1, 1]], axis=1)[None]


def solution(mesh):
    placed = (
        P("pipe", "dp", None),
        P("pipe", None),
        P("pipe", None, "dp", None),
        P("pipe", "dp", None),
    )
    return jax.shard_map(
        shards, mesh=mesh, in_specs=placed, out_specs=P("pipe", "dp", None), check_vma=False
    )
```

```python
import math

import jax
import jax.numpy as jnp
import numpy as np
from jax import lax
from jax.sharding import PartitionSpec as P

RING = 4
AXES = ("pipe", "dp")


def split_place(index):
    core = index % 2
    y = index // 2 % 4
    half_x = index // 8 % 2
    z = index // 16 % 4
    pipe = index // 64
    return pipe, z, half_x, y, core


def join_place(pipe, z, half_x, y, core):
    return (((pipe * 4 + z) * 2 + half_x) * 4 + y) * 2 + core


def send(value, pipe=0, z=0, x=0, y=0, core=0):
    pairs = []
    for source in range(128):
        p0, z0, x0, y0, c0 = split_place(source)
        target = join_place(p0 ^ pipe, (z0 + z) % 4, x0 ^ x, (y0 + y) % 4, c0 ^ core)
        pairs.append((source, target))
    return lax.ppermute(value, AXES, pairs)


def normalize(section_rows, gain_vector):
    values = section_rows.astype(jnp.float32)
    centre = jnp.mean(values, axis=-1, keepdims=True)
    shifted = values - centre
    spread = jnp.mean(shifted * shifted, axis=-1, keepdims=True)
    return (shifted * lax.rsqrt(spread + 1e-05) * gain_vector).astype(jnp.bfloat16)


def swap_pairs(axis, turn):
    pairs = []
    for source in range(128):
        pipe, z, half_x, y, core = split_place(source)
        flip = (1, 3)[turn ^ core]
        if axis == "z":
            z ^= flip
        else:
            y ^= flip
        pairs.append((source, join_place(pipe, z, half_x, y, core)))
    return pairs


def swap_both(first, first_axis, second, second_axis, turn, *beside):
    first, second = lax.optimization_barrier((first, second))
    first = lax.ppermute(first, AXES, swap_pairs(first_axis, turn))
    second = lax.ppermute(second, AXES, swap_pairs(second_axis, turn))
    return lax.optimization_barrier((first, second, *beside))


def near_rows(own, one, two, core):
    size = own.shape[0]
    return jnp.concatenate(
        [
            own,
            jnp.where(core == 0, one, two[:size]),
            jnp.where(core == 0, two[:size], one),
            two[size:],
        ]
    )


def swap_sum(first_far, first_near, second_far, second_near, first_axis, second_axis):
    size = first_far.shape[0] // 2
    first_got, second_got = swap_both(
        first_far.astype(jnp.bfloat16),
        first_axis,
        second_far.astype(jnp.bfloat16),
        second_axis,
        1,
    )
    first_sum = first_near + first_got.astype(jnp.float32)
    second_sum = second_near + second_got.astype(jnp.float32)
    first_got, second_got = swap_both(
        first_sum[size:].astype(jnp.bfloat16),
        first_axis,
        second_sum[size:].astype(jnp.bfloat16),
        second_axis,
        0,
    )
    return (
        first_sum[:size] + first_got.astype(jnp.float32),
        second_sum[:size] + second_got.astype(jnp.float32),
    )


def token_positions(z, y):
    places = np.asarray([0, 1, 3, 2], np.int32)
    far = np.repeat(places, 128)
    side = np.tile(np.repeat(np.asarray([0, 1], np.int32), 64), 4)
    near = np.tile(np.repeat(places, 16), 8)
    low = np.tile(np.arange(16, dtype=np.int32), 32)
    dz = np.where(side == 0, far, near)
    dy = np.where(side == 0, near, far)
    return (((z ^ dz) * 2 + side) * 4 + (y ^ dy)) * 16 + low


def attend(projected, position, head_size):
    queries = projected[:, :head_size]
    keys_part = projected[:, head_size : 2 * head_size]
    values_part = projected[:, 2 * head_size :].astype(jnp.bfloat16)
    scores = jnp.einsum(
        "qd,kd->qk", queries, keys_part, precision=lax.Precision.HIGHEST
    ) / math.sqrt(head_size)
    causal = position[:, None] >= position[None, :]
    scores = jnp.where(causal, scores, -1e30)
    largest = jnp.max(scores, axis=-1, keepdims=True)
    weights = jnp.where(causal, jnp.exp(scores - largest), 0.0)
    totals = jnp.sum(weights, axis=-1, keepdims=True)
    probabilities = (weights / totals).astype(jnp.bfloat16)
    return jnp.dot(probabilities, values_part, preferred_element_type=jnp.float32).astype(
        jnp.bfloat16
    )


def shards(segment_input, norm_gain, head_weights, output_weights):
    head_size = output_weights.shape[1]
    width = segment_input.shape[2]
    half, quarter = width // 2, width // 4
    _, z, half_x, y, core = split_place(lax.axis_index("dp"))

    normed = normalize(segment_input[0], norm_gain[0])
    left, right = normed[:, :half], normed[:, half:]
    kept = jnp.where(core == 0, left, right)
    given = send(jnp.where(core == 0, right, left), core=1)
    block = jnp.where(
        core == 0, jnp.concatenate([kept, given]), jnp.concatenate([given, kept])
    )
    head_block, block = lax.optimization_barrier((head_weights[0, :, 0, :], block))
    other = send(block, x=1)
    first = jnp.where(half_x == 0, block, other)
    second = jnp.where(half_x == 0, other, block)
    own_weights = lax.dynamic_slice_in_dim(head_block, core * half, half, 0)
    swapped_weights = send(
        lax.dynamic_slice_in_dim(head_block, (1 - core) * half, half, 0), core=1
    )

    one = swap_both(first, "y", second, "z", 0)
    two = swap_both(
        jnp.concatenate([first, one[0]]), "y", jnp.concatenate([second, one[1]]), "z", 1
    )
    first_far = [near_rows(first, one[0], two[0], core)]
    second_far = [near_rows(second, one[1], two[1], core)]

    out_rows, _ = lax.optimization_barrier((output_weights[0], two[0]))
    out_parts = []
    for dx, dc in ((0, 0), (0, 1), (1, 0), (1, 1)):
        start = ((half_x ^ dx) * 2 + (core ^ dc)) * quarter
        part = lax.dynamic_slice_in_dim(out_rows, start, quarter, 1)
        out_parts.append(send(part, x=dx, core=dc) if dx or dc else part)
    out_block = jnp.concatenate(out_parts, axis=0)

    def project(k):
        rows = jnp.concatenate([first_far[k], second_far[k]])
        mine = jnp.dot(rows, own_weights, preferred_element_type=jnp.float32)
        theirs = jnp.dot(rows, swapped_weights, preferred_element_type=jnp.float32)
        return mine, theirs

    here = [project(0)]
    for k, (source, turn) in enumerate(((0, 0), (0, 1), (1, 1))):
        got = swap_both(first_far[source], "z", second_far[source], "y", turn, *here[k])
        first_far.append(got[0])
        second_far.append(got[1])
        here[k] = got[2:]
        here.append(project(k + 1))
    by_place = [
        here[0],
        [jnp.where(core == 0, a, b) for a, b in zip(here[1], here[2])],
        [jnp.where(core == 0, b, a) for a, b in zip(here[1], here[2])],
        here[3],
    ]
    projected = jnp.concatenate([mine + send(theirs, core=1) for mine, theirs in by_place])

    attended = attend(projected, token_positions(z, y), head_size)
    across_x = send(attended, x=1)
    across_core = send(attended, core=1)
    across_both = send(across_x, core=1)
    heads = jnp.concatenate([attended, across_core, across_x, across_both], axis=1)

    def turns(blocks):
        middle = jnp.where(core == 0, blocks[2], blocks[1])
        kept = jnp.where(core == 0, blocks[1], blocks[2])
        return [middle, blocks[3]], [blocks[0], kept]

    heads = heads.reshape(4, 2, 64, 4 * head_size)
    first_sent, first_kept = turns(heads[:, 0])
    second_sent, second_kept = turns(heads[:, 1])
    edge = jnp.dot(
        jnp.concatenate(first_sent + second_sent),
        out_block,
        preferred_element_type=jnp.float32,
    ).astype(jnp.bfloat16)
    rest = jnp.dot(
        jnp.concatenate(first_kept + second_kept),
        out_block,
        preferred_element_type=jnp.float32,
    )
    first_sum, second_sum = swap_sum(
        edge[:128], rest[:128], edge[128:], rest[128:], "z", "y"
    )
    first_sent, first_kept = turns(first_sum.reshape(4, 16, quarter))
    second_sent, second_kept = turns(second_sum.reshape(4, 16, quarter))
    first_rows, second_rows = swap_sum(
        jnp.concatenate(first_sent),
        jnp.concatenate(first_kept),
        jnp.concatenate(second_sent),
        jnp.concatenate(second_kept),
        "y",
        "z",
    )
    owners = jnp.stack([first_rows, second_rows]).astype(jnp.bfloat16)
    upper, lower = owners[:, :8], owners[:, 8:]
    stay = jnp.where(core == 0, upper, lower)
    came = send(jnp.where(core == 0, lower, upper), core=1)
    wide = jnp.where(
        core == 0,
        jnp.concatenate([stay, came], axis=2),
        jnp.concatenate([came, stay], axis=2),
    )
    straight = send(jnp.where(half_x == 0, wide[0], wide[1]), pipe=1)
    crossed = send(jnp.where(half_x == 0, wide[1], wide[0]), pipe=1, x=1)
    return jnp.where(
        half_x == 0,
        jnp.concatenate([straight, crossed], axis=1),
        jnp.concatenate([crossed, straight], axis=1),
    )[None]


def solution(mesh):
    placed = (
        P("pipe", "dp", None),
        P("pipe", None),
        P("pipe", None, "dp", None),
        P("pipe", "dp", None),
    )
    return jax.shard_map(
        shards, mesh=mesh, in_specs=placed, out_specs=P("pipe", "dp", None), check_vma=False
    )
```

```python
import math

import jax
import jax.numpy as jnp
import numpy as np
from jax import lax
from jax.sharding import PartitionSpec as P

RING = 4
AXES = ("pipe", "dp")


def split_place(index):
    core = index % 2
    y = index // 2 % 4
    half_x = index // 8 % 2
    z = index // 16 % 4
    pipe = index // 64
    return pipe, z, half_x, y, core


def join_place(pipe, z, half_x, y, core):
    return (((pipe * 4 + z) * 2 + half_x) * 4 + y) * 2 + core


def send(value, pipe=0, z=0, x=0, y=0, core=0):
    pairs = []
    for source in range(128):
        p0, z0, x0, y0, c0 = split_place(source)
        target = join_place(p0 ^ pipe, (z0 + z) % 4, x0 ^ x, (y0 + y) % 4, c0 ^ core)
        pairs.append((source, target))
    return lax.ppermute(value, AXES, pairs)


def normalize(section_rows, gain_vector):
    values = section_rows.astype(jnp.float32)
    centre = jnp.mean(values, axis=-1, keepdims=True)
    shifted = values - centre
    spread = jnp.mean(shifted * shifted, axis=-1, keepdims=True)
    return (shifted * lax.rsqrt(spread + 1e-05) * gain_vector).astype(jnp.bfloat16)


def swap_pairs(axis, turn):
    pairs = []
    for source in range(128):
        pipe, z, half_x, y, core = split_place(source)
        flip = (1, 3)[turn ^ core]
        if axis == "z":
            z ^= flip
        else:
            y ^= flip
        pairs.append((source, join_place(pipe, z, half_x, y, core)))
    return pairs


def swap_both(first, first_axis, second, second_axis, turn, *beside):
    first, second = lax.optimization_barrier((first, second))
    first = lax.ppermute(first, AXES, swap_pairs(first_axis, turn))
    second = lax.ppermute(second, AXES, swap_pairs(second_axis, turn))
    return lax.optimization_barrier((first, second, *beside))


def near_rows(own, one, two, core):
    size = own.shape[0]
    return jnp.concatenate(
        [
            own,
            jnp.where(core == 0, one, two[:size]),
            jnp.where(core == 0, two[:size], one),
            two[size:],
        ]
    )


def swap_sum(first_far, first_near, second_far, second_near, first_axis, second_axis):
    size = first_far.shape[0] // 2
    first_got, second_got = swap_both(
        first_far.astype(jnp.bfloat16),
        first_axis,
        second_far.astype(jnp.bfloat16),
        second_axis,
        1,
    )
    first_sum = first_near + first_got.astype(jnp.float32)
    second_sum = second_near + second_got.astype(jnp.float32)
    first_got, second_got = swap_both(
        first_sum[size:].astype(jnp.bfloat16),
        first_axis,
        second_sum[size:].astype(jnp.bfloat16),
        second_axis,
        0,
    )
    return (
        first_sum[:size] + first_got.astype(jnp.float32),
        second_sum[:size] + second_got.astype(jnp.float32),
    )


def token_positions(z, y):
    places = np.asarray([0, 1, 3, 2], np.int32)
    far = np.repeat(places, 128)
    side = np.tile(np.repeat(np.asarray([0, 1], np.int32), 64), 4)
    near = np.tile(np.repeat(places, 16), 8)
    low = np.tile(np.arange(16, dtype=np.int32), 32)
    dz = np.where(side == 0, far, near)
    dy = np.where(side == 0, near, far)
    return (((z ^ dz) * 2 + side) * 4 + (y ^ dy)) * 16 + low


def attend(projected, position, head_size):
    queries = projected[:, :head_size]
    keys_part = projected[:, head_size : 2 * head_size]
    values_part = projected[:, 2 * head_size :].astype(jnp.bfloat16)
    scores = jnp.einsum(
        "qd,kd->qk", queries, keys_part, precision=lax.Precision.HIGHEST
    ) / math.sqrt(head_size)
    causal = position[:, None] >= position[None, :]
    scores = jnp.where(causal, scores, -1e30)
    largest = jnp.max(scores, axis=-1, keepdims=True)
    weights = jnp.where(causal, jnp.exp(scores - largest), 0.0)
    totals = jnp.sum(weights, axis=-1, keepdims=True)
    probabilities = (weights / totals).astype(jnp.bfloat16)
    return jnp.dot(probabilities, values_part, preferred_element_type=jnp.float32).astype(
        jnp.bfloat16
    )


def shards(segment_input, norm_gain, head_weights, output_weights):
    head_size = output_weights.shape[1]
    width = segment_input.shape[2]
    half, quarter = width // 2, width // 4
    _, z, half_x, y, core = split_place(lax.axis_index("dp"))

    normed = normalize(segment_input[0], norm_gain[0])
    left, right = normed[:, :half], normed[:, half:]
    kept = jnp.where(core == 0, left, right)
    given = send(jnp.where(core == 0, right, left), core=1)
    block = jnp.where(
        core == 0, jnp.concatenate([kept, given]), jnp.concatenate([given, kept])
    )
    head_block, block = lax.optimization_barrier((head_weights[0, :, 0, :], block))
    other, their_weights = lax.optimization_barrier(
        (
            send(block, x=1),
            lax.dynamic_slice_in_dim(head_block, (1 - core) * half, half, 0),
        )
    )
    first = jnp.where(half_x == 0, block, other)
    second = jnp.where(half_x == 0, other, block)
    own_weights = lax.dynamic_slice_in_dim(head_block, core * half, half, 0)

    out_rows, _ = lax.optimization_barrier((output_weights[0], block))
    *one, out_kept, out_given = swap_both(
        first,
        "y",
        second,
        "z",
        0,
        lax.dynamic_slice_in_dim(out_rows, half_x * half, half, 1),
        lax.dynamic_slice_in_dim(out_rows, (1 - half_x) * half, half, 1),
    )
    *two, swapped_weights = swap_both(
        jnp.concatenate([first, one[0]]),
        "y",
        jnp.concatenate([second, one[1]]),
        "z",
        1,
        send(their_weights, core=1),
    )
    first_own = near_rows(first, one[0], two[0], core)
    second_own = near_rows(second, one[1], two[1], core)

    def project(first_rows, second_rows):
        rows = jnp.concatenate([first_rows, second_rows])
        mine = jnp.dot(rows, own_weights, preferred_element_type=jnp.float32)
        theirs = jnp.dot(rows, swapped_weights, preferred_element_type=jnp.float32)
        return mine, theirs

    def swap_far(first_rows, second_rows, turn):
        return (
            lax.ppermute(first_rows, AXES, swap_pairs("z", turn)),
            lax.ppermute(second_rows, AXES, swap_pairs("y", turn)),
        )

    middle = out_given.shape[0] // 2
    first_own, second_own, upper, lower = lax.optimization_barrier(
        (first_own, second_own, out_given[:middle], out_given[middle:])
    )
    turn_one = swap_far(first_own, second_own, 0)
    turn_two = swap_far(first_own, second_own, 1)
    upper = send(upper, x=1)
    *turn_one, mine, theirs = lax.optimization_barrier(
        (*turn_one, *project(first_own, second_own))
    )
    here = [(mine, theirs)]
    *turn_one, upper, lower, mine, theirs, first_rows, second_rows = (
        lax.optimization_barrier((*turn_one, upper, lower, *project(*turn_one), *turn_two))
    )
    here.append((mine, theirs))
    last = swap_far(*turn_one, 1)
    here.append(project(first_rows, second_rows))
    lower, mine, theirs = lax.optimization_barrier((lower, *here[2]))
    here[2] = mine, theirs
    lower = send(lower, x=1)
    *last, mine, theirs = lax.optimization_barrier((*last, *here[2]))
    here[2] = mine, theirs
    here.append(project(*last))
    by_place = [
        here[0],
        [jnp.where(core == 0, a, b) for a, b in zip(here[1], here[2])],
        [jnp.where(core == 0, b, a) for a, b in zip(here[1], here[2])],
        here[3],
    ]
    projected = jnp.concatenate([mine + send(theirs, core=1) for mine, theirs in by_place])

    attended = attend(projected, token_positions(z, y), head_size)
    own_heads = jnp.concatenate([attended, send(attended, x=1)], axis=1)
    heads = jnp.concatenate([own_heads, send(own_heads, core=1)], axis=1)

    upper, lower, _ = lax.optimization_barrier((upper, lower, attended))
    out_halves = jnp.concatenate([out_kept, upper, lower])
    left, right = out_halves[:, :quarter], out_halves[:, quarter:]
    out_block = jnp.concatenate(
        [
            jnp.where(core == 0, left, right),
            send(jnp.where(core == 0, right, left), core=1),
        ]
    )

    def turns(blocks):
        middle = jnp.where(core == 0, blocks[2], blocks[1])
        kept = jnp.where(core == 0, blocks[1], blocks[2])
        return [middle, blocks[3]], [blocks[0], kept]

    heads = heads.reshape(4, 2, 64, 4 * head_size)
    first_sent, first_kept = turns(heads[:, 0])
    second_sent, second_kept = turns(heads[:, 1])
    edge = jnp.dot(
        jnp.concatenate(first_sent + second_sent),
        out_block,
        preferred_element_type=jnp.float32,
    ).astype(jnp.bfloat16)
    rest = jnp.dot(
        jnp.concatenate(first_kept + second_kept),
        out_block,
        preferred_element_type=jnp.float32,
    )
    first_sum, second_sum = swap_sum(
        edge[:128], rest[:128], edge[128:], rest[128:], "z", "y"
    )
    first_sent, first_kept = turns(first_sum.reshape(4, 16, quarter))
    second_sent, second_kept = turns(second_sum.reshape(4, 16, quarter))
    first_rows, second_rows = swap_sum(
        jnp.concatenate(first_sent),
        jnp.concatenate(first_kept),
        jnp.concatenate(second_sent),
        jnp.concatenate(second_kept),
        "y",
        "z",
    )
    owners = jnp.stack([first_rows, second_rows]).astype(jnp.bfloat16)
    upper, lower = owners[:, :8], owners[:, 8:]
    stay = jnp.where(core == 0, upper, lower)
    came = send(jnp.where(core == 0, lower, upper), core=1)
    wide = jnp.where(
        core == 0,
        jnp.concatenate([stay, came], axis=2),
        jnp.concatenate([came, stay], axis=2),
    )
    straight = send(jnp.where(half_x == 0, wide[0], wide[1]), pipe=1)
    crossed = send(jnp.where(half_x == 0, wide[1], wide[0]), pipe=1, x=1)
    return jnp.where(
        half_x == 0,
        jnp.concatenate([straight, crossed], axis=1),
        jnp.concatenate([crossed, straight], axis=1),
    )[None]


def solution(mesh):
    placed = (
        P("pipe", "dp", None),
        P("pipe", None),
        P("pipe", None, "dp", None),
        P("pipe", "dp", None),
    )
    return jax.shard_map(
        shards, mesh=mesh, in_specs=placed, out_specs=P("pipe", "dp", None), check_vma=False
    )
```

```python
import math

import jax
import jax.numpy as jnp
import numpy as np
from jax import lax
from jax.sharding import PartitionSpec as P

RING = 4
AXES = ("pipe", "dp")


def split_place(index):
    core = index % 2
    y = index // 2 % 4
    half_x = index // 8 % 2
    z = index // 16 % 4
    pipe = index // 64
    return pipe, z, half_x, y, core


def join_place(pipe, z, half_x, y, core):
    return (((pipe * 4 + z) * 2 + half_x) * 4 + y) * 2 + core


def send(value, pipe=0, z=0, x=0, y=0, core=0):
    pairs = []
    for source in range(128):
        p0, z0, x0, y0, c0 = split_place(source)
        target = join_place(p0 ^ pipe, (z0 + z) % 4, x0 ^ x, (y0 + y) % 4, c0 ^ core)
        pairs.append((source, target))
    return lax.ppermute(value, AXES, pairs)


def normalize(section_rows, gain_vector):
    values = section_rows.astype(jnp.float32)
    centre = jnp.mean(values, axis=-1, keepdims=True)
    shifted = values - centre
    spread = jnp.mean(shifted * shifted, axis=-1, keepdims=True)
    return (shifted * lax.rsqrt(spread + 1e-05) * gain_vector).astype(jnp.bfloat16)


def swap_pairs(axis, turn):
    pairs = []
    for source in range(128):
        pipe, z, half_x, y, core = split_place(source)
        flip = (1, 3)[turn ^ core]
        if axis == "z":
            z ^= flip
        else:
            y ^= flip
        pairs.append((source, join_place(pipe, z, half_x, y, core)))
    return pairs


def swap_both(first, first_axis, second, second_axis, turn):
    return (
        lax.ppermute(first, AXES, swap_pairs(first_axis, turn)),
        lax.ppermute(second, AXES, swap_pairs(second_axis, turn)),
    )


def near_rows(own, one, two, core):
    size = own.shape[0]
    return jnp.concatenate(
        [
            own,
            jnp.where(core == 0, one, two[:size]),
            jnp.where(core == 0, two[:size], one),
            two[size:],
        ]
    )


def swap_sum(far, near, axis):
    size = near.shape[0] // 2
    got = lax.ppermute(far.astype(jnp.bfloat16), AXES, swap_pairs(axis, 1))
    total = near + got.astype(jnp.float32)
    got = lax.ppermute(total[size:].astype(jnp.bfloat16), AXES, swap_pairs(axis, 0))
    return total[:size] + got.astype(jnp.float32)


def token_positions(z, y):
    places = np.asarray([0, 1, 3, 2], np.int32)
    far = np.repeat(places, 128)
    side = np.tile(np.repeat(np.asarray([0, 1], np.int32), 64), 4)
    near = np.tile(np.repeat(places, 16), 8)
    low = np.tile(np.arange(16, dtype=np.int32), 32)
    dz = np.where(side == 0, far, near)
    dy = np.where(side == 0, near, far)
    return (((z ^ dz) * 2 + side) * 4 + (y ^ dy)) * 16 + low


def attend(projected, position, head_size):
    queries = projected[:, :head_size]
    keys_part = projected[:, head_size : 2 * head_size]
    values_part = projected[:, 2 * head_size :].astype(jnp.bfloat16)
    scores = jnp.einsum(
        "qd,kd->qk", queries, keys_part, precision=lax.Precision.HIGHEST
    ) / math.sqrt(head_size)
    causal = position[:, None] >= position[None, :]
    scores = jnp.where(causal, scores, -1e30)
    largest = jnp.max(scores, axis=-1, keepdims=True)
    weights = jnp.where(causal, jnp.exp(scores - largest), 0.0)
    totals = jnp.sum(weights, axis=-1, keepdims=True)
    probabilities = (weights / totals).astype(jnp.bfloat16)
    return jnp.dot(probabilities, values_part, preferred_element_type=jnp.float32).astype(
        jnp.bfloat16
    )


def shards(segment_input, norm_gain, head_weights, output_weights):
    head_size = output_weights.shape[1]
    width = segment_input.shape[2]
    half, quarter = width // 2, width // 4
    _, z, half_x, y, core = split_place(lax.axis_index("dp"))

    normed = normalize(segment_input[0], norm_gain[0])
    left, right = normed[:, :half], normed[:, half:]
    kept = jnp.where(core == 0, left, right)
    given = send(jnp.where(core == 0, right, left), core=1)
    block = jnp.where(
        core == 0, jnp.concatenate([kept, given]), jnp.concatenate([given, kept])
    )
    head_block, block = lax.optimization_barrier((head_weights[0, :, 0, :], block))
    other, their_weights = lax.optimization_barrier(
        (
            send(block, x=1),
            lax.dynamic_slice_in_dim(head_block, (1 - core) * half, half, 0),
        )
    )
    first = jnp.where(half_x == 0, block, other)
    second = jnp.where(half_x == 0, other, block)
    own_weights = lax.dynamic_slice_in_dim(head_block, core * half, half, 0)

    one = swap_both(first, "y", second, "z", 0)
    two = swap_both(
        jnp.concatenate([first, one[0]]), "y", jnp.concatenate([second, one[1]]), "z", 1
    )
    first_own = near_rows(first, one[0], two[0], core)
    second_own = near_rows(second, one[1], two[1], core)
    swapped_weights = send(their_weights, core=1)

    out_rows, _ = lax.optimization_barrier((output_weights[0], block))
    out_kept = lax.dynamic_slice_in_dim(out_rows, half_x * half, half, 1)
    out_given = lax.dynamic_slice_in_dim(out_rows, (1 - half_x) * half, half, 1)
    middle = out_given.shape[0] // 2
    upper, _ = lax.optimization_barrier((out_given[:middle], one))
    upper = send(upper, x=1)

    def project(first_rows, second_rows):
        rows = jnp.concatenate([first_rows, second_rows])
        mine = jnp.dot(rows, own_weights, preferred_element_type=jnp.float32)
        theirs = jnp.dot(rows, swapped_weights, preferred_element_type=jnp.float32)
        return mine, theirs

    first_own, second_own = lax.optimization_barrier((first_own, second_own))
    turn_one = swap_both(first_own, "z", second_own, "y", 0)
    turn_two = swap_both(first_own, "z", second_own, "y", 1)
    *turn_one, upper, mine, theirs = lax.optimization_barrier(
        (*turn_one, upper, *project(first_own, second_own))
    )
    here = [(mine, theirs)]
    lower, _ = lax.optimization_barrier((out_given[middle:], upper))
    lower = send(lower, x=1)
    *turn_one, first_rows, second_rows = lax.optimization_barrier((*turn_one, *turn_two))
    last = swap_both(turn_one[0], "z", turn_one[1], "y", 1)
    here.append(project(*turn_one))
    here.append(project(first_rows, second_rows))
    *last, middle_sums = lax.optimization_barrier((*last, here[1:]))
    here[1:] = middle_sums
    here.append(project(*last))
    by_place = [
        here[0],
        [jnp.where(core == 0, a, b) for a, b in zip(here[1], here[2])],
        [jnp.where(core == 0, b, a) for a, b in zip(here[1], here[2])],
        here[3],
    ]
    projected = jnp.concatenate([mine + send(theirs, core=1) for mine, theirs in by_place])

    attended = attend(projected, token_positions(z, y), head_size)
    own_heads = jnp.concatenate([attended, send(attended, x=1)], axis=1)
    heads = jnp.concatenate([own_heads, send(own_heads, core=1)], axis=1)

    def swap_quarters(rows):
        left, right = rows[:, :quarter], rows[:, quarter:]
        given = send(jnp.where(core == 0, right, left), core=1)
        return jnp.where(core == 0, left, right), given

    lower, _ = lax.optimization_barrier((lower, attended))
    out_block = jnp.concatenate(
        [
            jnp.concatenate(pieces)
            for pieces in zip(
                swap_quarters(jnp.concatenate([out_kept, upper])), swap_quarters(lower)
            )
        ]
    )

    def turns(blocks):
        middle = jnp.where(core == 0, blocks[2], blocks[1])
        kept = jnp.where(core == 0, blocks[1], blocks[2])
        return [middle, blocks[3]], [blocks[0], kept]

    heads = heads.reshape(4, 2, 64, 4 * head_size)

    def section_rows(side, far_axis, near_axis):
        sent, kept = turns(heads[:, side])
        edge = jnp.dot(
            jnp.concatenate(sent), out_block, preferred_element_type=jnp.float32
        ).astype(jnp.bfloat16)
        rest = jnp.dot(jnp.concatenate(kept), out_block, preferred_element_type=jnp.float32)
        total = swap_sum(edge, lax.optimization_barrier(rest), far_axis)
        sent, kept = turns(total.reshape(4, 16, quarter))
        return swap_sum(jnp.concatenate(sent), jnp.concatenate(kept), near_axis)

    first_rows = section_rows(0, "z", "y")
    second_rows = section_rows(1, "y", "z")
    owners = jnp.stack([first_rows, second_rows]).astype(jnp.bfloat16)
    upper, lower = owners[:, :8], owners[:, 8:]
    stay = jnp.where(core == 0, upper, lower)
    came = send(jnp.where(core == 0, lower, upper), core=1)
    wide = jnp.where(
        core == 0,
        jnp.concatenate([stay, came], axis=2),
        jnp.concatenate([came, stay], axis=2),
    )
    straight = send(jnp.where(half_x == 0, wide[0], wide[1]), pipe=1)
    crossed = send(jnp.where(half_x == 0, wide[1], wide[0]), pipe=1, x=1)
    return jnp.where(
        half_x == 0,
        jnp.concatenate([straight, crossed], axis=1),
        jnp.concatenate([crossed, straight], axis=1),
    )[None]


def solution(mesh):
    placed = (
        P("pipe", "dp", None),
        P("pipe", None),
        P("pipe", None, "dp", None),
        P("pipe", "dp", None),
    )
    return jax.shard_map(
        shards, mesh=mesh, in_specs=placed, out_specs=P("pipe", "dp", None), check_vma=False
    )
```

```python
import math

import jax
import jax.numpy as jnp
import numpy as np
from jax import lax
from jax.sharding import PartitionSpec as P

RING = 4
AXES = ("pipe", "dp")


def split_place(index):
    core = index % 2
    y = index // 2 % 4
    half_x = index // 8 % 2
    z = index // 16 % 4
    pipe = index // 64
    return pipe, z, half_x, y, core


def join_place(pipe, z, half_x, y, core):
    return (((pipe * 4 + z) * 2 + half_x) * 4 + y) * 2 + core


def send(value, pipe=0, z=0, x=0, y=0, core=0):
    pairs = []
    for source in range(128):
        p0, z0, x0, y0, c0 = split_place(source)
        target = join_place(p0 ^ pipe, (z0 + z) % 4, x0 ^ x, (y0 + y) % 4, c0 ^ core)
        pairs.append((source, target))
    return lax.ppermute(value, AXES, pairs)


def normalize(section_rows, gain_vector):
    values = section_rows.astype(jnp.float32)
    centre = jnp.mean(values, axis=-1, keepdims=True)
    shifted = values - centre
    spread = jnp.mean(shifted * shifted, axis=-1, keepdims=True)
    return (shifted * lax.rsqrt(spread + 1e-05) * gain_vector).astype(jnp.bfloat16)


def swap_pairs(axis, turn):
    pairs = []
    for source in range(128):
        pipe, z, half_x, y, core = split_place(source)
        flip = (1, 3)[turn ^ core]
        if axis == "z":
            z ^= flip
        else:
            y ^= flip
        pairs.append((source, join_place(pipe, z, half_x, y, core)))
    return pairs


def swap_both(first, first_axis, second, second_axis, turn):
    return (
        lax.ppermute(first, AXES, swap_pairs(first_axis, turn)),
        lax.ppermute(second, AXES, swap_pairs(second_axis, turn)),
    )


def near_rows(own, one, two, core):
    size = own.shape[0]
    return jnp.concatenate(
        [
            own,
            jnp.where(core == 0, one, two[:size]),
            jnp.where(core == 0, two[:size], one),
            two[size:],
        ]
    )


def swap_sum(far, near, axis, *ready):
    size = near.shape[0] // 2
    got = lax.ppermute(far.astype(jnp.bfloat16), AXES, swap_pairs(axis, 1))
    total = near + got.astype(jnp.float32)
    kept, got = total[:size], lax.ppermute(
        total[size:].astype(jnp.bfloat16), AXES, swap_pairs(axis, 0)
    )
    kept, *_ = lax.optimization_barrier((kept, *ready))
    return kept + got.astype(jnp.float32)


def token_positions(z, half_x, y):
    places = np.asarray([0, 1, 3, 2], np.int32)
    far = np.repeat(places, 128)
    side = np.tile(np.repeat(np.asarray([0, 1], np.int32), 64), 4)
    near = np.tile(np.repeat(places, 16), 8)
    low = np.tile(np.arange(16, dtype=np.int32), 32)
    dz = np.where(side == 0, far, near)
    dy = np.where(side == 0, near, far)
    return (((z ^ dz) * 2 + (half_x ^ side)) * 4 + (y ^ dy)) * 16 + low


def attend(projected, position, head_size):
    queries = projected[:, :head_size]
    keys_part = projected[:, head_size : 2 * head_size]
    values_part = projected[:, 2 * head_size :].astype(jnp.bfloat16)
    scores = jnp.einsum(
        "qd,kd->qk", queries, keys_part, precision=lax.Precision.HIGHEST
    ) / math.sqrt(head_size)
    causal = position[:, None] >= position[None, :]
    scores = jnp.where(causal, scores, -1e30)
    largest = jnp.max(scores, axis=-1, keepdims=True)
    weights = jnp.where(causal, jnp.exp(scores - largest), 0.0)
    totals = jnp.sum(weights, axis=-1, keepdims=True)
    probabilities = (weights / totals).astype(jnp.bfloat16)
    return jnp.dot(probabilities, values_part, preferred_element_type=jnp.float32).astype(
        jnp.bfloat16
    )


def shards(segment_input, norm_gain, head_weights, output_weights):
    head_size = output_weights.shape[1]
    width = segment_input.shape[2]
    half, quarter = width // 2, width // 4
    _, z, half_x, y, core = split_place(lax.axis_index("dp"))

    normed = normalize(segment_input[0], norm_gain[0])
    left, right = normed[:, :half], normed[:, half:]
    kept = jnp.where(core == 0, left, right)
    given = send(jnp.where(core == 0, right, left), core=1)
    block = jnp.where(
        core == 0, jnp.concatenate([kept, given]), jnp.concatenate([given, kept])
    )
    head_block, block = lax.optimization_barrier((head_weights[0, :, 0, :], block))
    first, second = block, send(block, x=1)
    their_weights = lax.dynamic_slice_in_dim(head_block, (1 - core) * half, half, 0)
    swapped_weights = send(their_weights, core=1)
    own_weights = lax.dynamic_slice_in_dim(head_block, core * half, half, 0)

    def near_gather(block, axis):
        one = lax.ppermute(block, AXES, swap_pairs(axis, 0))
        two = lax.ppermute(jnp.concatenate([block, one]), AXES, swap_pairs(axis, 1))
        return lax.optimization_barrier(near_rows(block, one, two, core)), one

    first_own, _ = near_gather(first, "y")
    second_own, came = near_gather(second, "z")
    second_own, swapped_weights = lax.optimization_barrier((second_own, swapped_weights))

    out_rows, _ = lax.optimization_barrier((output_weights[0], block))
    out_kept = lax.dynamic_slice_in_dim(out_rows, half_x * half, half, 1)
    out_given = lax.dynamic_slice_in_dim(out_rows, (1 - half_x) * half, half, 1)
    middle = out_given.shape[0] // 2
    upper, _ = lax.optimization_barrier((out_given[:middle], came))
    upper = send(upper, x=1)

    def project(first_rows, second_rows):
        rows = jnp.concatenate([first_rows, second_rows])
        mine = jnp.dot(rows, own_weights, preferred_element_type=jnp.float32)
        theirs = jnp.dot(rows, swapped_weights, preferred_element_type=jnp.float32)
        return mine, theirs

    turn_one = swap_both(first_own, "z", second_own, "y", 0)
    turn_two = swap_both(first_own, "z", second_own, "y", 1)
    last = swap_both(turn_one[0], "z", turn_one[1], "y", 1)
    here = [project(first_own, second_own)]
    lower, _ = lax.optimization_barrier((out_given[middle:], upper))
    lower = send(lower, x=1)
    here.append(project(*turn_one))
    here.append(project(*turn_two))
    *last, here = lax.optimization_barrier((*last, here))
    here.append(project(*last))
    by_place = [
        here[0],
        [jnp.where(core == 0, a, b) for a, b in zip(here[1], here[2])],
        [jnp.where(core == 0, b, a) for a, b in zip(here[1], here[2])],
        here[3],
    ]
    projected = jnp.concatenate([mine + send(theirs, core=1) for mine, theirs in by_place])

    attended = attend(projected, token_positions(z, half_x, y), head_size)
    across_x = send(attended, x=1).reshape(4, 2, 4, 16, head_size)
    across_x = jnp.flip(across_x, 1).transpose(2, 1, 0, 3, 4)
    own_heads = jnp.concatenate([attended, across_x.reshape(attended.shape)], axis=1)
    heads = jnp.concatenate([own_heads, send(own_heads, core=1)], axis=1)

    def swap_quarters(rows):
        left, right = rows[:, :quarter], rows[:, quarter:]
        given = send(jnp.where(core == 0, right, left), core=1)
        return jnp.where(core == 0, left, right), given

    lower, _ = lax.optimization_barrier((lower, attended))
    out_block = jnp.concatenate(
        [
            jnp.concatenate(pieces)
            for pieces in zip(
                swap_quarters(jnp.concatenate([out_kept, upper])), swap_quarters(lower)
            )
        ]
    )

    def turns(blocks):
        middle = jnp.where(core == 0, blocks[2], blocks[1])
        kept = jnp.where(core == 0, blocks[1], blocks[2])
        return [middle, blocks[3]], [blocks[0], kept]

    heads = heads.reshape(4, 2, 64, 4 * head_size)

    def edge_and_rest(side):
        sent, kept = turns(heads[:, side])
        edge = jnp.dot(
            jnp.concatenate(sent), out_block, preferred_element_type=jnp.float32
        ).astype(jnp.bfloat16)
        rest = jnp.dot(jnp.concatenate(kept), out_block, preferred_element_type=jnp.float32)
        return edge, lax.optimization_barrier(rest)

    def near_chunks(total):
        sent, kept = turns(lax.optimization_barrier(total).reshape(4, 16, quarter))
        return jnp.concatenate(sent).astype(jnp.bfloat16), jnp.concatenate(kept)

    first_sent, first_kept = near_chunks(swap_sum(*edge_and_rest(0), "z"))
    second_sent, second_kept = near_chunks(swap_sum(*edge_and_rest(1), "y", first_sent))
    first_rows = swap_sum(first_sent, first_kept, "y")
    second_rows = swap_sum(second_sent, second_kept, "z")
    owners = jnp.stack([first_rows, second_rows]).astype(jnp.bfloat16)
    upper, lower = owners[:, :8], owners[:, 8:]
    stay = jnp.where(core == 0, upper, lower)
    came = send(jnp.where(core == 0, lower, upper), core=1)
    wide = jnp.where(
        core == 0,
        jnp.concatenate([stay, came], axis=2),
        jnp.concatenate([came, stay], axis=2),
    )
    straight = send(wide[0], pipe=1)
    crossed = send(wide[1], pipe=1, x=1)
    return jnp.where(
        half_x == 0,
        jnp.concatenate([straight, crossed], axis=1),
        jnp.concatenate([crossed, straight], axis=1),
    )[None]


def solution(mesh):
    placed = (
        P("pipe", "dp", None),
        P("pipe", None),
        P("pipe", None, "dp", None),
        P("pipe", "dp", None),
    )
    return jax.shard_map(
        shards, mesh=mesh, in_specs=placed, out_specs=P("pipe", "dp", None), check_vma=False
    )
```

```python
import math

import jax
import jax.numpy as jnp
import numpy as np
from jax import lax
from jax.sharding import PartitionSpec as P

RING = 4
AXES = ("pipe", "dp")


def split_place(index):
    core = index % 2
    y = index // 2 % 4
    half_x = index // 8 % 2
    z = index // 16 % 4
    pipe = index // 64
    return pipe, z, half_x, y, core


def join_place(pipe, z, half_x, y, core):
    return (((pipe * 4 + z) * 2 + half_x) * 4 + y) * 2 + core


def send(value, pipe=0, z=0, x=0, y=0, core=0):
    pairs = []
    for source in range(128):
        p0, z0, x0, y0, c0 = split_place(source)
        target = join_place(p0 ^ pipe, (z0 + z) % 4, x0 ^ x, (y0 + y) % 4, c0 ^ core)
        pairs.append((source, target))
    return lax.ppermute(value, AXES, pairs)


def normalize(section_rows, gain_vector):
    values = section_rows.astype(jnp.float32)
    centre = jnp.mean(values, axis=-1, keepdims=True)
    shifted = values - centre
    spread = jnp.mean(shifted * shifted, axis=-1, keepdims=True)
    return (shifted * lax.rsqrt(spread + 1e-05) * gain_vector).astype(jnp.bfloat16)


def swap_pairs(axis, turn):
    pairs = []
    for source in range(128):
        pipe, z, half_x, y, core = split_place(source)
        flip = (1, 3)[turn ^ core]
        if axis == "z":
            z ^= flip
        else:
            y ^= flip
        pairs.append((source, join_place(pipe, z, half_x, y, core)))
    return pairs


def swap_both(first, first_axis, second, second_axis, turn):
    return (
        lax.ppermute(first, AXES, swap_pairs(first_axis, turn)),
        lax.ppermute(second, AXES, swap_pairs(second_axis, turn)),
    )


def near_rows(own, one, two, core):
    size = own.shape[0]
    return jnp.concatenate(
        [
            own,
            jnp.where(core == 0, one, two[:size]),
            jnp.where(core == 0, two[:size], one),
            two[size:],
        ]
    )


def swap_sum(far, near, axis):
    size = near.shape[0] // 2
    got = lax.ppermute(far.astype(jnp.bfloat16), AXES, swap_pairs(axis, 1))
    total = near + got.astype(jnp.float32)
    got = lax.ppermute(total[size:].astype(jnp.bfloat16), AXES, swap_pairs(axis, 0))
    return total[:size] + got.astype(jnp.float32)


def token_positions(z, y):
    places = np.asarray([0, 1, 3, 2], np.int32)
    far = np.repeat(places, 128)
    side = np.tile(np.repeat(np.asarray([0, 1], np.int32), 64), 4)
    near = np.tile(np.repeat(places, 16), 8)
    low = np.tile(np.arange(16, dtype=np.int32), 32)
    dz = np.where(side == 0, far, near)
    dy = np.where(side == 0, near, far)
    return (((z ^ dz) * 2 + side) * 4 + (y ^ dy)) * 16 + low


def attend(projected, position, head_size):
    queries = projected[:, :head_size]
    keys_part = projected[:, head_size : 2 * head_size]
    values_part = projected[:, 2 * head_size :].astype(jnp.bfloat16)
    scores = jnp.einsum(
        "qd,kd->qk", queries, keys_part, precision=lax.Precision.HIGHEST
    ) / math.sqrt(head_size)
    causal = position[:, None] >= position[None, :]
    scores = jnp.where(causal, scores, -1e30)
    largest = jnp.max(scores, axis=-1, keepdims=True)
    weights = jnp.where(causal, jnp.exp(scores - largest), 0.0)
    totals = jnp.sum(weights, axis=-1, keepdims=True)
    probabilities = (weights / totals).astype(jnp.bfloat16)
    return jnp.dot(probabilities, values_part, preferred_element_type=jnp.float32).astype(
        jnp.bfloat16
    )


def shards(segment_input, norm_gain, head_weights, output_weights):
    head_size = output_weights.shape[1]
    width = segment_input.shape[2]
    half, quarter = width // 2, width // 4
    _, z, half_x, y, core = split_place(lax.axis_index("dp"))

    normed = normalize(segment_input[0], norm_gain[0])
    left, right = normed[:, :half], normed[:, half:]
    kept = jnp.where(core == 0, left, right)
    given = send(jnp.where(core == 0, right, left), core=1)
    block = jnp.where(
        core == 0, jnp.concatenate([kept, given]), jnp.concatenate([given, kept])
    )
    head_block, block = lax.optimization_barrier((head_weights[0, :, 0, :], block))
    other, their_weights = lax.optimization_barrier(
        (
            send(block, x=1),
            lax.dynamic_slice_in_dim(head_block, (1 - core) * half, half, 0),
        )
    )
    first = jnp.where(half_x == 0, block, other)
    second = jnp.where(half_x == 0, other, block)
    own_weights = lax.dynamic_slice_in_dim(head_block, core * half, half, 0)

    one = swap_both(first, "y", second, "z", 0)
    two = swap_both(
        jnp.concatenate([first, one[0]]), "y", jnp.concatenate([second, one[1]]), "z", 1
    )
    first_own = near_rows(first, one[0], two[0], core)
    second_own = near_rows(second, one[1], two[1], core)
    swapped_weights = send(their_weights, core=1)

    out_rows, _ = lax.optimization_barrier((output_weights[0], block))
    out_kept = lax.dynamic_slice_in_dim(out_rows, half_x * half, half, 1)
    out_given = lax.dynamic_slice_in_dim(out_rows, (1 - half_x) * half, half, 1)
    middle = out_given.shape[0] // 2
    upper, _ = lax.optimization_barrier((out_given[:middle], one))
    upper = send(upper, x=1)
    first_own, second_own, swapped_weights = lax.optimization_barrier(
        (first_own, second_own, swapped_weights)
    )

    def project(first_rows, second_rows, weights):
        rows = jnp.concatenate([first_rows, second_rows])
        return jnp.dot(rows, weights, preferred_element_type=jnp.float32)

    turn_one = swap_both(first_own, "z", second_own, "y", 0)
    mine = [project(first_own, second_own, own_weights)]
    first_late, second_late, mine[0] = lax.optimization_barrier(
        (first_own, second_own, mine[0])
    )
    turn_two = swap_both(first_late, "z", second_late, "y", 1)
    theirs = [project(first_own, second_own, swapped_weights)]
    turn_one, upper, theirs = lax.optimization_barrier((turn_one, upper, theirs))
    last = swap_both(turn_one[0], "z", turn_one[1], "y", 1)
    mine.append(project(*turn_one, own_weights))
    theirs.append(project(*turn_one, swapped_weights))
    lower, near_block, _ = lax.optimization_barrier(
        (out_given[middle:], jnp.concatenate([out_kept, upper]), theirs)
    )
    lower = send(lower, x=1)
    near_crossed = send(near_block, core=1)
    last, mine, theirs, turn_two = lax.optimization_barrier((last, mine, theirs, turn_two))
    for rows in (turn_two, last):
        mine.append(project(*rows, own_weights))
        theirs.append(project(*rows, swapped_weights))
    here = list(zip(mine, theirs))
    by_place = [
        here[0],
        [jnp.where(core == 0, a, b) for a, b in zip(here[1], here[2])],
        [jnp.where(core == 0, b, a) for a, b in zip(here[1], here[2])],
        here[3],
    ]
    projected = jnp.concatenate([mine + send(theirs, core=1) for mine, theirs in by_place])

    attended = attend(projected, token_positions(z, y), head_size)
    own_heads = jnp.concatenate([attended, send(attended, x=1)], axis=1)
    by_core = own_heads.reshape(32, 2, 8, 2 * head_size)
    upper_rows, lower_rows = by_core[:, 0], by_core[:, 1]
    kept_heads = jnp.where(core == 0, upper_rows, lower_rows)
    given_heads = send(jnp.where(core == 0, lower_rows, upper_rows), core=1)
    heads = jnp.concatenate([kept_heads, given_heads], axis=2)

    lower, near_crossed, _ = lax.optimization_barrier((lower, near_crossed, attended))
    out_block = jnp.concatenate([near_block, lower, near_crossed, send(lower, core=1)])

    def turns(blocks):
        middle = jnp.where(core == 0, blocks[2], blocks[1])
        kept = jnp.where(core == 0, blocks[1], blocks[2])
        return [middle, blocks[3]], [blocks[0], kept]

    heads = heads.reshape(4, 2, 32, 4 * head_size)

    def out_rows_of(blocks):
        return jnp.dot(
            jnp.concatenate(blocks), out_block, preferred_element_type=jnp.float32
        )

    first_sent, first_kept = turns(heads[:, 0])
    second_sent, second_kept = turns(heads[:, 1])
    edges = out_rows_of(first_sent + second_sent).astype(jnp.bfloat16)
    rests = lax.optimization_barrier(out_rows_of(first_kept + second_kept))
    edges, rests = edges.reshape(2, 64, half), rests.reshape(2, 64, half)

    def section_rows(side, far_axis, near_axis):
        total = swap_sum(edges[side], rests[side], far_axis)
        sent, kept = turns(total.reshape(4, 8, half))
        return swap_sum(jnp.concatenate(sent), jnp.concatenate(kept), near_axis)

    first_rows = section_rows(0, "z", "y").astype(jnp.bfloat16)
    second_rows = section_rows(1, "y", "z").astype(jnp.bfloat16)
    straight = send(jnp.where(half_x == 0, first_rows, second_rows), pipe=1)
    crossed = send(jnp.where(half_x == 0, second_rows, first_rows), pipe=1, x=1)
    return jnp.where(
        half_x == 0,
        jnp.concatenate([straight, crossed], axis=1),
        jnp.concatenate([crossed, straight], axis=1),
    )[None]


def solution(mesh):
    placed = (
        P("pipe", "dp", None),
        P("pipe", None),
        P("pipe", None, "dp", None),
        P("pipe", "dp", None),
    )
    return jax.shard_map(
        shards, mesh=mesh, in_specs=placed, out_specs=P("pipe", "dp", None), check_vma=False
    )
```

```python
import math

import jax
import jax.numpy as jnp
import numpy as np
from jax import lax
from jax.experimental import pallas as pl
from jax.experimental.pallas import tpu as pltpu
from jax.sharding import PartitionSpec as P

RING = 4
AXES = ("pipe", "dp")


def split_place(index):
    core = index % 2
    y = index // 2 % 4
    half_x = index // 8 % 2
    z = index // 16 % 4
    pipe = index // 64
    return pipe, z, half_x, y, core


def join_place(pipe, z, half_x, y, core):
    return (((pipe * 4 + z) * 2 + half_x) * 4 + y) * 2 + core


def send(value, pipe=0, z=0, x=0, y=0, core=0):
    pairs = []
    for source in range(128):
        p0, z0, x0, y0, c0 = split_place(source)
        target = join_place(p0 ^ pipe, (z0 + z) % 4, x0 ^ x, (y0 + y) % 4, c0 ^ core)
        pairs.append((source, target))
    return lax.ppermute(value, AXES, pairs)


def normalize_rows(core_ref, rows_ref, gain_ref, kept_ref, given_ref):
    values = rows_ref[...].astype(jnp.float32)
    centre = jnp.mean(values, axis=-1, keepdims=True)
    shifted = values - centre
    spread = jnp.mean(shifted * shifted, axis=-1, keepdims=True)
    normed = (shifted * lax.rsqrt(spread + 1e-05) * gain_ref[...]).astype(jnp.bfloat16)
    half = kept_ref.shape[1]

    @pl.when(core_ref[0] == 0)
    def _():
        kept_ref[...] = normed[:, :half]
        given_ref[...] = normed[:, half:]

    @pl.when(core_ref[0] != 0)
    def _():
        kept_ref[...] = normed[:, half:]
        given_ref[...] = normed[:, :half]


def normalize(section_rows, gain_vector, core):
    count, width = section_rows.shape
    part = jax.ShapeDtypeStruct((count, width // 2), jnp.bfloat16)
    whole = pl.BlockSpec(memory_space=pltpu.VMEM)
    return pl.pallas_call(
        normalize_rows,
        out_shape=(part, part),
        in_specs=[pl.BlockSpec(memory_space=pltpu.SMEM), whole, whole],
        out_specs=(whole, whole),
    )(jnp.reshape(core, (1,)), section_rows, gain_vector)


def swap_pairs(axis, turn):
    pairs = []
    for source in range(128):
        pipe, z, half_x, y, core = split_place(source)
        flip = (1, 3)[turn ^ core]
        if axis == "z":
            z ^= flip
        else:
            y ^= flip
        pairs.append((source, join_place(pipe, z, half_x, y, core)))
    return pairs


def swap_both(first, first_axis, second, second_axis, turn):
    return (
        lax.ppermute(first, AXES, swap_pairs(first_axis, turn)),
        lax.ppermute(second, AXES, swap_pairs(second_axis, turn)),
    )


def near_rows(own, one, two, core):
    size = own.shape[0]
    return jnp.concatenate(
        [
            own,
            jnp.where(core == 0, one, two[:size]),
            jnp.where(core == 0, two[:size], one),
            two[size:],
        ]
    )


def swap_sums(fars, nears, axes):
    size = nears[0].shape[0] // 2
    fars = lax.optimization_barrier([far.astype(jnp.bfloat16) for far in fars])
    got = lax.optimization_barrier(swap_both(fars[0], axes[0], fars[1], axes[1], 1))
    totals = [near + part.astype(jnp.float32) for near, part in zip(nears, got)]
    sent = lax.optimization_barrier(
        [total[size:].astype(jnp.bfloat16) for total in totals]
    )
    got = lax.optimization_barrier(swap_both(sent[0], axes[0], sent[1], axes[1], 0))
    return [total[:size] + part.astype(jnp.float32) for total, part in zip(totals, got)]


def token_positions(z, y):
    places = np.asarray([0, 1, 3, 2], np.int32)
    far = np.repeat(places, 128)
    side = np.tile(np.repeat(np.asarray([0, 1], np.int32), 64), 4)
    near = np.tile(np.repeat(places, 16), 8)
    low = np.tile(np.arange(16, dtype=np.int32), 32)
    dz = np.where(side == 0, far, near)
    dy = np.where(side == 0, near, far)
    return (((z ^ dz) * 2 + side) * 4 + (y ^ dy)) * 16 + low


def attend(projected, position, head_size):
    queries = projected[:, :head_size]
    keys_part = projected[:, head_size : 2 * head_size]
    values_part = projected[:, 2 * head_size :].astype(jnp.bfloat16)
    scores = jnp.einsum(
        "qd,kd->qk", queries, keys_part, precision=lax.Precision.HIGHEST
    ) / math.sqrt(head_size)
    causal = position[:, None] >= position[None, :]
    scores = jnp.where(causal, scores, -1e30)
    largest = jnp.max(scores, axis=-1, keepdims=True)
    weights = jnp.where(causal, jnp.exp(scores - largest), 0.0)
    totals = jnp.sum(weights, axis=-1, keepdims=True)
    probabilities = (weights / totals).astype(jnp.bfloat16)
    return jnp.dot(probabilities, values_part, preferred_element_type=jnp.float32).astype(
        jnp.bfloat16
    )


def shards(segment_input, norm_gain, head_weights, output_weights):
    head_size = output_weights.shape[1]
    width = segment_input.shape[2]
    half, quarter = width // 2, width // 4
    _, z, half_x, y, core = split_place(lax.axis_index("dp"))

    kept, given = normalize(segment_input[0], norm_gain, core)
    given = send(given, core=1)
    block = jnp.where(
        core == 0, jnp.concatenate([kept, given]), jnp.concatenate([given, kept])
    )
    head_block, block = lax.optimization_barrier((head_weights[0, :, 0, :], block))
    other, their_weights = lax.optimization_barrier(
        (
            send(block, x=1),
            lax.dynamic_slice_in_dim(head_block, (1 - core) * half, half, 0),
        )
    )
    first = jnp.where(half_x == 0, block, other)
    second = jnp.where(half_x == 0, other, block)
    own_weights = lax.dynamic_slice_in_dim(head_block, core * half, half, 0)

    one = swap_both(first, "y", second, "z", 0)
    two = swap_both(
        jnp.concatenate([first, one[0]]), "y", jnp.concatenate([second, one[1]]), "z", 1
    )
    first_own = near_rows(first, one[0], two[0], core)
    second_own = near_rows(second, one[1], two[1], core)
    swapped_weights = send(their_weights, core=1)

    out_rows, _ = lax.optimization_barrier((output_weights[0], block))
    out_kept = lax.dynamic_slice_in_dim(out_rows, half_x * half, half, 1)
    out_given = lax.dynamic_slice_in_dim(out_rows, (1 - half_x) * half, half, 1)
    out_given, _ = lax.optimization_barrier((out_given, one))
    out_across = send(out_given, x=1)

    def project(first_rows, second_rows):
        rows = jnp.concatenate([first_rows, second_rows])
        mine = jnp.dot(rows, own_weights, preferred_element_type=jnp.float32)
        theirs = jnp.dot(rows, swapped_weights, preferred_element_type=jnp.float32)
        return mine, theirs

    first_own, second_own, swapped_weights = lax.optimization_barrier(
        (first_own, second_own, swapped_weights)
    )
    turn_one = swap_both(first_own, "z", second_own, "y", 0)
    turn_two = swap_both(first_own, "z", second_own, "y", 1)
    here = [project(first_own, second_own)]
    turn_one, turn_two, here = lax.optimization_barrier((turn_one, turn_two, here))
    last = swap_both(turn_one[0], "z", turn_one[1], "y", 1)
    here.append(project(*turn_one))
    here.append(project(*turn_two))
    out_across, _ = lax.optimization_barrier((out_across, here))
    near_block = jnp.concatenate([out_kept, out_across])
    near_crossed = send(near_block, core=1)
    last, here = lax.optimization_barrier((last, here))
    here.append(project(*last))
    by_place = [
        here[0],
        [jnp.where(core == 0, a, b) for a, b in zip(here[1], here[2])],
        [jnp.where(core == 0, b, a) for a, b in zip(here[1], here[2])],
        here[3],
    ]
    projected = jnp.concatenate([mine + send(theirs, core=1) for mine, theirs in by_place])

    attended = attend(projected, token_positions(z, y), head_size)
    own_heads = jnp.concatenate([attended, send(attended, x=1)], axis=1)
    by_core = own_heads.reshape(32, 2, 8, 2 * head_size)
    upper_rows, lower_rows = by_core[:, 0], by_core[:, 1]
    kept_heads = jnp.where(core == 0, upper_rows, lower_rows)
    given_heads = send(jnp.where(core == 0, lower_rows, upper_rows), core=1)
    heads = jnp.concatenate([kept_heads, given_heads], axis=2)

    out_block = jnp.concatenate([near_block, near_crossed])

    def turns(blocks):
        middle = jnp.where(core == 0, blocks[2], blocks[1])
        kept = jnp.where(core == 0, blocks[1], blocks[2])
        return [middle, blocks[3]], [blocks[0], kept]

    heads = heads.reshape(4, 2, 32, 4 * head_size)

    def out_rows_of(blocks):
        return jnp.dot(
            jnp.concatenate(blocks), out_block, preferred_element_type=jnp.float32
        )

    first_sent, first_kept = turns(heads[:, 0])
    second_sent, second_kept = turns(heads[:, 1])
    edges = out_rows_of(first_sent + second_sent).astype(jnp.bfloat16)
    rests = lax.optimization_barrier(out_rows_of(first_kept + second_kept))
    size = edges.shape[0] // 2
    totals = swap_sums(
        (edges[:size], edges[size:]), (rests[:size], rests[size:]), ("z", "y")
    )
    chunks = [turns(total.reshape(4, -1, half)) for total in totals]
    first_rows, second_rows = swap_sums(
        [jnp.concatenate(sent) for sent, _ in chunks],
        [jnp.concatenate(kept) for _, kept in chunks],
        ("y", "z"),
    )
    first_rows = first_rows.astype(jnp.bfloat16)
    second_rows = second_rows.astype(jnp.bfloat16)
    straight = send(jnp.where(half_x == 0, first_rows, second_rows), pipe=1)
    crossed = send(jnp.where(half_x == 0, second_rows, first_rows), pipe=1, x=1)
    return jnp.where(
        half_x == 0,
        jnp.concatenate([straight, crossed], axis=1),
        jnp.concatenate([crossed, straight], axis=1),
    )[None]


def solution(mesh):
    placed = (
        P("pipe", "dp", None),
        P("pipe", None),
        P("pipe", None, "dp", None),
        P("pipe", "dp", None),
    )
    return jax.shard_map(
        shards, mesh=mesh, in_specs=placed, out_specs=P("pipe", "dp", None), check_vma=False
    )
```

```python
import math

import jax
import jax.numpy as jnp
import numpy as np
from jax import lax
from jax.experimental import pallas as pl
from jax.experimental.layout import Layout, with_layout_constraint
from jax.experimental.pallas import tpu as pltpu
from jax.sharding import PartitionSpec as P

RING = 4
AXES = ("pipe", "dp")


def split_place(index):
    core = index % 2
    y = index // 2 % 4
    half_x = index // 8 % 2
    z = index // 16 % 4
    pipe = index // 64
    return pipe, z, half_x, y, core


def join_place(pipe, z, half_x, y, core):
    return (((pipe * 4 + z) * 2 + half_x) * 4 + y) * 2 + core


def send(value, pipe=0, z=0, x=0, y=0, core=0):
    pairs = []
    for source in range(128):
        p0, z0, x0, y0, c0 = split_place(source)
        target = join_place(p0 ^ pipe, (z0 + z) % 4, x0 ^ x, (y0 + y) % 4, c0 ^ core)
        pairs.append((source, target))
    return lax.ppermute(value, AXES, pairs)


def normalize_rows(core_ref, rows_ref, gain_ref, kept_ref, given_ref):
    values = rows_ref[...].astype(jnp.float32)
    centre = jnp.mean(values, axis=-1, keepdims=True)
    shifted = values - centre
    spread = jnp.mean(shifted * shifted, axis=-1, keepdims=True)
    normed = (shifted * lax.rsqrt(spread + 1e-05) * gain_ref[...]).astype(jnp.bfloat16)
    half = kept_ref.shape[1]

    @pl.when(core_ref[0] == 0)
    def _():
        kept_ref[...] = normed[:, :half]
        given_ref[...] = normed[:, half:]

    @pl.when(core_ref[0] != 0)
    def _():
        kept_ref[...] = normed[:, half:]
        given_ref[...] = normed[:, :half]


def normalize(section_rows, gain_vector, core):
    count, width = section_rows.shape
    part = pltpu.VMEM((count, width // 2), jnp.bfloat16)
    whole = pl.BlockSpec(memory_space=pltpu.VMEM)
    return pl.pallas_call(
        normalize_rows,
        out_shape=(part, part),
        in_specs=[pl.BlockSpec(memory_space=pltpu.SMEM), whole, whole],
        out_specs=(whole, whole),
    )(jnp.reshape(core, (1,)), section_rows, gain_vector)


def swap_pairs(axis, turn):
    pairs = []
    for source in range(128):
        pipe, z, half_x, y, core = split_place(source)
        flip = (1, 3)[turn ^ core]
        if axis == "z":
            z ^= flip
        else:
            y ^= flip
        pairs.append((source, join_place(pipe, z, half_x, y, core)))
    return pairs


def swap_both(first, first_axis, second, second_axis, turn):
    return (
        lax.ppermute(first, AXES, swap_pairs(first_axis, turn)),
        lax.ppermute(second, AXES, swap_pairs(second_axis, turn)),
    )


def near_rows(own, one, two, core):
    size = own.shape[0]
    return jnp.concatenate(
        [
            own,
            jnp.where(core == 0, one, two[:size]),
            jnp.where(core == 0, two[:size], one),
            two[size:],
        ]
    )


def swap_sums(fars, nears, axes):
    size = nears[0].shape[0] // 2
    fars = lax.optimization_barrier([far.astype(jnp.bfloat16) for far in fars])
    got = lax.optimization_barrier(swap_both(fars[0], axes[0], fars[1], axes[1], 1))
    totals = [near + part.astype(jnp.float32) for near, part in zip(nears, got)]
    sent = lax.optimization_barrier(
        [total[size:].astype(jnp.bfloat16) for total in totals]
    )
    got = lax.optimization_barrier(swap_both(sent[0], axes[0], sent[1], axes[1], 0))
    return [total[:size] + part.astype(jnp.float32) for total, part in zip(totals, got)]


def token_positions(z, y):
    places = np.asarray([0, 1, 3, 2], np.int32)
    far = np.repeat(places, 128)
    side = np.tile(np.repeat(np.asarray([0, 1], np.int32), 64), 4)
    near = np.tile(np.repeat(places, 16), 8)
    low = np.tile(np.arange(16, dtype=np.int32), 32)
    dz = np.where(side == 0, far, near)
    dy = np.where(side == 0, near, far)
    return (((z ^ dz) * 2 + side) * 4 + (y ^ dy)) * 16 + low


def attend(projected, position, head_size):
    queries = projected[:, :head_size]
    keys_part = projected[:, head_size : 2 * head_size]
    values_part = projected[:, 2 * head_size :].astype(jnp.bfloat16)
    scores = jnp.einsum(
        "qd,kd->qk", queries, keys_part, precision=lax.Precision.HIGHEST
    ) / math.sqrt(head_size)
    causal = position[:, None] >= position[None, :]
    scores = jnp.where(causal, scores, -1e30)
    largest = jnp.max(scores, axis=-1, keepdims=True)
    weights = jnp.where(causal, jnp.exp(scores - largest), 0.0)
    totals = jnp.sum(weights, axis=-1, keepdims=True)
    probabilities = (weights / totals).astype(jnp.bfloat16)
    return jnp.dot(probabilities, values_part, preferred_element_type=jnp.float32).astype(
        jnp.bfloat16
    )


def shards(segment_input, norm_gain, head_weights, output_weights):
    head_size = output_weights.shape[1]
    width = segment_input.shape[2]
    half, quarter = width // 2, width // 4
    _, z, half_x, y, core = split_place(lax.axis_index("dp"))

    kept, given = normalize(segment_input[0], norm_gain, core)
    given = send(given, core=1)
    block = jnp.where(
        core == 0, jnp.concatenate([kept, given]), jnp.concatenate([given, kept])
    )
    head_block, block = lax.optimization_barrier((head_weights[0, :, 0, :], block))
    other, their_weights = lax.optimization_barrier(
        (
            send(block, x=1),
            lax.dynamic_slice_in_dim(head_block, (1 - core) * half, half, 0),
        )
    )
    first = jnp.where(half_x == 0, block, other)
    second = jnp.where(half_x == 0, other, block)
    own_weights = lax.dynamic_slice_in_dim(head_block, core * half, half, 0)

    one = swap_both(first, "y", second, "z", 0)
    two = swap_both(
        jnp.concatenate([first, one[0]]), "y", jnp.concatenate([second, one[1]]), "z", 1
    )
    first_own = near_rows(first, one[0], two[0], core)
    second_own = near_rows(second, one[1], two[1], core)
    swapped_weights = send(their_weights, core=1)

    out_rows, _ = lax.optimization_barrier((output_weights[0], block))
    out_kept = lax.dynamic_slice_in_dim(out_rows, half_x * half, half, 1)
    out_given = lax.dynamic_slice_in_dim(out_rows, (1 - half_x) * half, half, 1)
    out_given, _ = lax.optimization_barrier((out_given, one))
    out_across = send(out_given, x=1)

    def project(first_rows, second_rows):
        rows = jnp.concatenate([first_rows, second_rows])
        mine = jnp.dot(rows, own_weights, preferred_element_type=jnp.float32)
        theirs = jnp.dot(rows, swapped_weights, preferred_element_type=jnp.float32)
        return mine, theirs

    first_own, second_own, swapped_weights = lax.optimization_barrier(
        (first_own, second_own, swapped_weights)
    )
    turn_one = swap_both(first_own, "z", second_own, "y", 0)
    turn_two = swap_both(first_own, "z", second_own, "y", 1)
    here = [project(first_own, second_own)]
    turn_one, turn_two, here = lax.optimization_barrier((turn_one, turn_two, here))
    last = swap_both(turn_one[0], "z", turn_one[1], "y", 1)
    here.append(project(*turn_one))
    here.append(project(*turn_two))
    out_across, _ = lax.optimization_barrier((out_across, here))
    near_block = jnp.concatenate([out_kept, out_across])
    near_crossed = send(near_block, core=1)
    last, here = lax.optimization_barrier((last, here))
    here.append(project(*last))
    by_place = [
        here[0],
        [jnp.where(core == 0, a, b) for a, b in zip(here[1], here[2])],
        [jnp.where(core == 0, b, a) for a, b in zip(here[1], here[2])],
        here[3],
    ]
    projected = jnp.concatenate([mine + send(theirs, core=1) for mine, theirs in by_place])

    attended = with_layout_constraint(
        attend(projected, token_positions(z, y), head_size), Layout(major_to_minor=(0, 1))
    )
    across = send(attended, x=1)
    out_block, across = lax.optimization_barrier(
        (jnp.concatenate([near_block, near_crossed]), across)
    )

    def of_core(rows, place):
        by_core = rows.reshape(32, 2, 8, head_size)
        return jnp.where(place == 0, by_core[:, 0], by_core[:, 1])

    given_heads = send(
        jnp.concatenate([of_core(attended, 1 - core), of_core(across, 1 - core)], axis=2),
        core=1,
    )
    heads = jnp.concatenate(
        [of_core(attended, core), of_core(across, core), given_heads], axis=2
    )

    def turns(blocks):
        middle = jnp.where(core == 0, blocks[2], blocks[1])
        kept = jnp.where(core == 0, blocks[1], blocks[2])
        return [middle, blocks[3]], [blocks[0], kept]

    heads = heads.reshape(4, 2, 32, 4 * head_size)

    def out_rows_of(blocks):
        return jnp.dot(
            jnp.concatenate(blocks), out_block, preferred_element_type=jnp.float32
        )

    first_sent, first_kept = turns(heads[:, 0])
    second_sent, second_kept = turns(heads[:, 1])
    edges = out_rows_of(first_sent + second_sent).astype(jnp.bfloat16)
    rests = lax.optimization_barrier(out_rows_of(first_kept + second_kept))
    size = edges.shape[0] // 2
    totals = swap_sums(
        (edges[:size], edges[size:]), (rests[:size], rests[size:]), ("z", "y")
    )
    chunks = [turns(total.reshape(4, -1, half)) for total in totals]
    first_rows, second_rows = swap_sums(
        [jnp.concatenate(sent) for sent, _ in chunks],
        [jnp.concatenate(kept) for _, kept in chunks],
        ("y", "z"),
    )
    first_rows = first_rows.astype(jnp.bfloat16)
    second_rows = second_rows.astype(jnp.bfloat16)
    straight = send(jnp.where(half_x == 0, first_rows, second_rows), pipe=1)
    crossed = send(jnp.where(half_x == 0, second_rows, first_rows), pipe=1, x=1)
    return jnp.where(
        half_x == 0,
        jnp.concatenate([straight, crossed], axis=1),
        jnp.concatenate([crossed, straight], axis=1),
    )[None]


def solution(mesh):
    placed = (
        P("pipe", "dp", None),
        P("pipe", None),
        P("pipe", None, "dp", None),
        P("pipe", "dp", None),
    )
    return jax.shard_map(
        shards, mesh=mesh, in_specs=placed, out_specs=P("pipe", "dp", None), check_vma=False
    )
```

```python
import math

import jax
import jax.numpy as jnp
import numpy as np
from jax import lax
from jax.experimental import pallas as pl
from jax.experimental.layout import Layout, with_layout_constraint
from jax.experimental.pallas import tpu as pltpu
from jax.sharding import PartitionSpec as P

RING = 4
AXES = ("pipe", "dp")


def split_place(index):
    core = index % 2
    y = index // 2 % 4
    half_x = index // 8 % 2
    z = index // 16 % 4
    pipe = index // 64
    return pipe, z, half_x, y, core


def join_place(pipe, z, half_x, y, core):
    return (((pipe * 4 + z) * 2 + half_x) * 4 + y) * 2 + core


def send(value, pipe=0, z=0, x=0, y=0, core=0):
    pairs = []
    for source in range(128):
        p0, z0, x0, y0, c0 = split_place(source)
        target = join_place(p0 ^ pipe, (z0 + z) % 4, x0 ^ x, (y0 + y) % 4, c0 ^ core)
        pairs.append((source, target))
    return lax.ppermute(value, AXES, pairs)


def normalize_rows(core_ref, rows_ref, gain_ref, kept_ref, given_ref):
    values = rows_ref[...].astype(jnp.float32)
    centre = jnp.mean(values, axis=-1, keepdims=True)
    shifted = values - centre
    spread = jnp.mean(shifted * shifted, axis=-1, keepdims=True)
    normed = (shifted * lax.rsqrt(spread + 1e-05) * gain_ref[...]).astype(jnp.bfloat16)
    half = kept_ref.shape[1]

    @pl.when(core_ref[0] == 0)
    def _():
        kept_ref[...] = normed[:, :half]
        given_ref[...] = normed[:, half:]

    @pl.when(core_ref[0] != 0)
    def _():
        kept_ref[...] = normed[:, half:]
        given_ref[...] = normed[:, :half]


def normalize(section_rows, gain_vector, core):
    count, width = section_rows.shape
    part = pltpu.VMEM((count, width // 2), jnp.bfloat16)
    whole = pl.BlockSpec(memory_space=pltpu.VMEM)
    return pl.pallas_call(
        normalize_rows,
        out_shape=(part, part),
        in_specs=[pl.BlockSpec(memory_space=pltpu.SMEM), whole, whole],
        out_specs=(whole, whole),
    )(jnp.reshape(core, (1,)), section_rows, gain_vector)


def swap_pairs(axis, turn):
    pairs = []
    for source in range(128):
        pipe, z, half_x, y, core = split_place(source)
        flip = (1, 3)[turn ^ core]
        if axis == "z":
            z ^= flip
        else:
            y ^= flip
        pairs.append((source, join_place(pipe, z, half_x, y, core)))
    return pairs


def swap_both(first, first_axis, second, second_axis, turn):
    return (
        lax.ppermute(first, AXES, swap_pairs(first_axis, turn)),
        lax.ppermute(second, AXES, swap_pairs(second_axis, turn)),
    )


def near_rows(own, one, two, core):
    size = own.shape[0]
    return jnp.concatenate(
        [
            own,
            jnp.where(core == 0, one, two[:size]),
            jnp.where(core == 0, two[:size], one),
            two[size:],
        ]
    )


def swap_sums(fars, nears, axes):
    size = nears[0].shape[0] // 2
    fars = lax.optimization_barrier([far.astype(jnp.bfloat16) for far in fars])
    got = lax.optimization_barrier(swap_both(fars[0], axes[0], fars[1], axes[1], 1))
    totals = [near + part.astype(jnp.float32) for near, part in zip(nears, got)]
    sent = lax.optimization_barrier(
        [total[size:].astype(jnp.bfloat16) for total in totals]
    )
    got = lax.optimization_barrier(swap_both(sent[0], axes[0], sent[1], axes[1], 0))
    return [total[:size] + part.astype(jnp.float32) for total, part in zip(totals, got)]


def token_positions(z, y):
    places = np.asarray([0, 1, 3, 2], np.int32)
    far = np.repeat(places, 128)
    side = np.tile(np.repeat(np.asarray([0, 1], np.int32), 64), 4)
    near = np.tile(np.repeat(places, 16), 8)
    low = np.tile(np.arange(16, dtype=np.int32), 32)
    dz = np.where(side == 0, far, near)
    dy = np.where(side == 0, near, far)
    return (((z ^ dz) * 2 + side) * 4 + (y ^ dy)) * 16 + low


def attend(projected, position, head_size):
    queries = projected[:, :head_size]
    keys_part = projected[:, head_size : 2 * head_size]
    values_part = projected[:, 2 * head_size :].astype(jnp.bfloat16)
    scores = jnp.einsum(
        "qd,kd->qk", queries, keys_part, precision=lax.Precision.HIGHEST
    ) / math.sqrt(head_size)
    causal = position[:, None] >= position[None, :]
    scores = jnp.where(causal, scores, -1e30)
    largest = jnp.max(scores, axis=-1, keepdims=True)
    weights = jnp.where(causal, jnp.exp(scores - largest), 0.0)
    totals = jnp.sum(weights, axis=-1, keepdims=True)
    probabilities = (weights / totals).astype(jnp.bfloat16)
    return jnp.dot(probabilities, values_part, preferred_element_type=jnp.float32).astype(
        jnp.bfloat16
    )


def shards(segment_input, norm_gain, head_weights, output_weights):
    head_size = output_weights.shape[1]
    width = segment_input.shape[2]
    half, quarter = width // 2, width // 4
    _, z, half_x, y, core = split_place(lax.axis_index("dp"))

    kept, given = normalize(segment_input[0], norm_gain, core)
    given = send(given, core=1)
    block = jnp.where(
        core == 0, jnp.concatenate([kept, given]), jnp.concatenate([given, kept])
    )
    head_block, block = lax.optimization_barrier((head_weights[0, :, 0, :], block))
    other = send(block, x=1)
    their_weights = lax.dynamic_slice_in_dim(head_block, (1 - core) * half, half, 0)
    swapped_weights = send(their_weights, core=1)
    first = jnp.where(half_x == 0, block, other)
    second = jnp.where(half_x == 0, other, block)
    own_weights = lax.dynamic_slice_in_dim(head_block, core * half, half, 0)

    one = swap_both(first, "y", second, "z", 0)
    two = swap_both(
        jnp.concatenate([first, one[0]]), "y", jnp.concatenate([second, one[1]]), "z", 1
    )
    first_own = near_rows(first, one[0], two[0], core)
    second_own = near_rows(second, one[1], two[1], core)

    out_rows, _ = lax.optimization_barrier((output_weights[0], block))
    out_kept = lax.dynamic_slice_in_dim(out_rows, half_x * half, half, 1)
    out_given = lax.dynamic_slice_in_dim(out_rows, (1 - half_x) * half, half, 1)
    out_given, _ = lax.optimization_barrier((out_given, one))
    out_across = send(out_given, x=1)

    def project(first_rows, second_rows):
        rows = jnp.concatenate([first_rows, second_rows])
        mine = jnp.dot(rows, own_weights, preferred_element_type=jnp.float32)
        theirs = jnp.dot(rows, swapped_weights, preferred_element_type=jnp.float32)
        return mine, theirs

    first_own, second_own, swapped_weights = lax.optimization_barrier(
        (first_own, second_own, swapped_weights)
    )
    turn_one = swap_both(first_own, "z", second_own, "y", 0)
    turn_two = swap_both(first_own, "z", second_own, "y", 1)
    here = [project(first_own, second_own)]
    turn_one, turn_two, here = lax.optimization_barrier((turn_one, turn_two, here))
    last = swap_both(turn_one[0], "z", turn_one[1], "y", 1)
    here.append(project(*turn_one))
    here.append(project(*turn_two))
    out_across, _ = lax.optimization_barrier((out_across, here))
    near_block = jnp.concatenate([out_kept, out_across])
    near_crossed = send(near_block, core=1)
    sums = [
        mine + send(theirs, core=1)
        for mine, theirs in (
            here[0],
            [jnp.where(core == 0, a, b) for a, b in zip(here[1], here[2])],
            [jnp.where(core == 0, b, a) for a, b in zip(here[1], here[2])],
        )
    ]
    last, sums = lax.optimization_barrier((last, sums))
    mine, theirs = project(*last)
    sums.append(lax.optimization_barrier(mine) + send(theirs, core=1))
    projected = jnp.concatenate(sums)

    attended = with_layout_constraint(
        attend(projected, token_positions(z, y), head_size), Layout(major_to_minor=(0, 1))
    )
    across = send(attended, x=1)
    out_block, across = lax.optimization_barrier(
        (jnp.concatenate([near_block, near_crossed]), across)
    )

    def of_core(rows, place):
        by_core = rows.reshape(32, 2, 8, head_size)
        return jnp.where(place == 0, by_core[:, 0], by_core[:, 1])

    given_heads = send(
        jnp.concatenate([of_core(attended, 1 - core), of_core(across, 1 - core)], axis=2),
        core=1,
    )
    heads = jnp.concatenate(
        [of_core(attended, core), of_core(across, core), given_heads], axis=2
    )

    def turns(blocks):
        middle = jnp.where(core == 0, blocks[2], blocks[1])
        kept = jnp.where(core == 0, blocks[1], blocks[2])
        return [middle, blocks[3]], [blocks[0], kept]

    heads = heads.reshape(4, 2, 32, 4 * head_size)

    def out_rows_of(blocks):
        return jnp.dot(
            jnp.concatenate(blocks), out_block, preferred_element_type=jnp.float32
        )

    first_sent, first_kept = turns(heads[:, 0])
    second_sent, second_kept = turns(heads[:, 1])
    edges = out_rows_of(first_sent + second_sent).astype(jnp.bfloat16)
    rests = lax.optimization_barrier(out_rows_of(first_kept + second_kept))
    size = edges.shape[0] // 2
    totals = swap_sums(
        (edges[:size], edges[size:]), (rests[:size], rests[size:]), ("z", "y")
    )
    chunks = [turns(total.reshape(4, -1, half)) for total in totals]
    first_rows, second_rows = swap_sums(
        [jnp.concatenate(sent) for sent, _ in chunks],
        [jnp.concatenate(kept) for _, kept in chunks],
        ("y", "z"),
    )
    first_rows = first_rows.astype(jnp.bfloat16)
    second_rows = second_rows.astype(jnp.bfloat16)
    straight = send(jnp.where(half_x == 0, first_rows, second_rows), pipe=1)
    crossed = send(jnp.where(half_x == 0, second_rows, first_rows), pipe=1, x=1)
    return jnp.where(
        half_x == 0,
        jnp.concatenate([straight, crossed], axis=1),
        jnp.concatenate([crossed, straight], axis=1),
    )[None]


def solution(mesh):
    placed = (
        P("pipe", "dp", None),
        P("pipe", None),
        P("pipe", None, "dp", None),
        P("pipe", "dp", None),
    )
    return jax.shard_map(
        shards, mesh=mesh, in_specs=placed, out_specs=P("pipe", "dp", None), check_vma=False
    )
```

```python
import math

import jax
import jax.numpy as jnp
import numpy as np
from jax import lax
from jax.experimental import pallas as pl
from jax.experimental.layout import Layout, with_layout_constraint
from jax.experimental.pallas import tpu as pltpu
from jax.sharding import PartitionSpec as P

RING = 4
AXES = ("pipe", "dp")


def split_place(index):
    core = index % 2
    y = index // 2 % 4
    half_x = index // 8 % 2
    z = index // 16 % 4
    pipe = index // 64
    return pipe, z, half_x, y, core


def join_place(pipe, z, half_x, y, core):
    return (((pipe * 4 + z) * 2 + half_x) * 4 + y) * 2 + core


def send(value, pipe=0, z=0, x=0, y=0, core=0):
    pairs = []
    for source in range(128):
        p0, z0, x0, y0, c0 = split_place(source)
        target = join_place(p0 ^ pipe, (z0 + z) % 4, x0 ^ x, (y0 + y) % 4, c0 ^ core)
        pairs.append((source, target))
    return lax.ppermute(value, AXES, pairs)


def normalize_rows(core_ref, rows_ref, gain_ref, kept_ref, given_ref):
    values = rows_ref[...].astype(jnp.float32)
    centre = jnp.mean(values, axis=-1, keepdims=True)
    shifted = values - centre
    spread = jnp.mean(shifted * shifted, axis=-1, keepdims=True)
    normed = (shifted * lax.rsqrt(spread + 1e-05) * gain_ref[...]).astype(jnp.bfloat16)
    half = kept_ref.shape[1]

    @pl.when(core_ref[0] == 0)
    def _():
        kept_ref[...] = normed[:, :half]
        given_ref[...] = normed[:, half:]

    @pl.when(core_ref[0] != 0)
    def _():
        kept_ref[...] = normed[:, half:]
        given_ref[...] = normed[:, :half]


def normalize(section_rows, gain_vector, core):
    count, width = section_rows.shape
    part = pltpu.VMEM((count, width // 2), jnp.bfloat16)
    whole = pl.BlockSpec(memory_space=pltpu.VMEM)
    return pl.pallas_call(
        normalize_rows,
        out_shape=(part, part),
        in_specs=[pl.BlockSpec(memory_space=pltpu.SMEM), whole, whole],
        out_specs=(whole, whole),
    )(jnp.reshape(core, (1,)), section_rows, gain_vector)


def swap_pairs(axis, turn):
    pairs = []
    for source in range(128):
        pipe, z, half_x, y, core = split_place(source)
        flip = (1, 3)[turn ^ core]
        if axis == "z":
            z ^= flip
        else:
            y ^= flip
        pairs.append((source, join_place(pipe, z, half_x, y, core)))
    return pairs


def swap_both(first, first_axis, second, second_axis, turn):
    return (
        lax.ppermute(first, AXES, swap_pairs(first_axis, turn)),
        lax.ppermute(second, AXES, swap_pairs(second_axis, turn)),
    )


def near_rows(own, one, two, core):
    size = own.shape[0]
    return jnp.concatenate(
        [
            own,
            jnp.where(core == 0, one, two[:size]),
            jnp.where(core == 0, two[:size], one),
            two[size:],
        ]
    )


def halve_sums(fars, nears, axes, turn):
    fars = lax.optimization_barrier([far.astype(jnp.bfloat16) for far in fars])
    got = lax.optimization_barrier(swap_both(fars[0], axes[0], fars[1], axes[1], turn))
    return [near + part.astype(jnp.float32) for near, part in zip(nears, got)]


def owner_pairs(crossed, near):
    pairs = []
    for source in range(128):
        pipe, z, half_x, y, core = split_place(source)
        half_x ^= crossed
        flip = (1, 3)[core] if near else 0
        if half_x:
            z ^= flip
        else:
            y ^= flip
        pairs.append((source, join_place(1 - pipe, z, half_x, y, core)))
    return pairs


def token_positions(z, y):
    places = np.asarray([0, 1, 3, 2], np.int32)
    far = np.repeat(places, 128)
    side = np.tile(np.repeat(np.asarray([0, 1], np.int32), 64), 4)
    near = np.tile(np.repeat(places, 16), 8)
    low = np.tile(np.arange(16, dtype=np.int32), 32)
    dz = np.where(side == 0, far, near)
    dy = np.where(side == 0, near, far)
    return (((z ^ dz) * 2 + side) * 4 + (y ^ dy)) * 16 + low


def attend(projected, position, head_size):
    queries = projected[:, :head_size]
    keys_part = projected[:, head_size : 2 * head_size]
    values_part = projected[:, 2 * head_size :].astype(jnp.bfloat16)
    scores = jnp.einsum(
        "qd,kd->qk", queries, keys_part, precision=lax.Precision.HIGHEST
    ) / math.sqrt(head_size)
    causal = position[:, None] >= position[None, :]
    scores = jnp.where(causal, scores, -1e30)
    largest = jnp.max(scores, axis=-1, keepdims=True)
    weights = jnp.where(causal, jnp.exp(scores - largest), 0.0)
    totals = jnp.sum(weights, axis=-1, keepdims=True)
    probabilities = (weights / totals).astype(jnp.bfloat16)
    return jnp.dot(probabilities, values_part, preferred_element_type=jnp.float32).astype(
        jnp.bfloat16
    )


def shards(segment_input, norm_gain, head_weights, output_weights):
    head_size = output_weights.shape[1]
    width = segment_input.shape[2]
    half, quarter = width // 2, width // 4
    _, z, half_x, y, core = split_place(lax.axis_index("dp"))

    kept, given = normalize(segment_input[0], norm_gain, core)
    given = send(given, core=1)
    block = jnp.where(
        core == 0, jnp.concatenate([kept, given]), jnp.concatenate([given, kept])
    )
    head_block, block = lax.optimization_barrier((head_weights[0, :, 0, :], block))
    other = send(block, x=1)
    their_weights = lax.dynamic_slice_in_dim(head_block, (1 - core) * half, half, 0)
    swapped_weights = send(their_weights, core=1)
    first = jnp.where(half_x == 0, block, other)
    second = jnp.where(half_x == 0, other, block)
    own_weights = lax.dynamic_slice_in_dim(head_block, core * half, half, 0)

    one = swap_both(first, "y", second, "z", 0)
    two = swap_both(
        jnp.concatenate([first, one[0]]), "y", jnp.concatenate([second, one[1]]), "z", 1
    )
    first_own = near_rows(first, one[0], two[0], core)
    second_own = near_rows(second, one[1], two[1], core)

    out_rows, _ = lax.optimization_barrier((output_weights[0], block))
    out_kept = lax.dynamic_slice_in_dim(out_rows, half_x * half, half, 1)
    out_given = lax.dynamic_slice_in_dim(out_rows, (1 - half_x) * half, half, 1)
    out_given, _ = lax.optimization_barrier((out_given, one))
    out_across = send(out_given, x=1)

    def project(first_rows, second_rows):
        rows = jnp.concatenate([first_rows, second_rows])
        mine = jnp.dot(rows, own_weights, preferred_element_type=jnp.float32)
        theirs = jnp.dot(rows, swapped_weights, preferred_element_type=jnp.float32)
        return mine, theirs

    first_own, second_own, swapped_weights = lax.optimization_barrier(
        (first_own, second_own, swapped_weights)
    )
    turn_one = swap_both(first_own, "z", second_own, "y", 0)
    turn_two = swap_both(first_own, "z", second_own, "y", 1)
    here = [project(first_own, second_own)]
    turn_one, turn_two, here = lax.optimization_barrier((turn_one, turn_two, here))
    last = swap_both(turn_one[0], "z", turn_one[1], "y", 1)
    here.append(project(*turn_one))
    here.append(project(*turn_two))
    out_across, _ = lax.optimization_barrier((out_across, here))
    near_block = jnp.concatenate([out_kept, out_across])
    near_crossed = send(near_block, core=1)
    sums = [
        mine + send(theirs, core=1)
        for mine, theirs in (
            here[0],
            [jnp.where(core == 0, a, b) for a, b in zip(here[1], here[2])],
            [jnp.where(core == 0, b, a) for a, b in zip(here[1], here[2])],
        )
    ]
    last, sums = lax.optimization_barrier((last, sums))
    mine, theirs = project(*last)
    sums.append(lax.optimization_barrier(mine) + send(theirs, core=1))
    projected = jnp.concatenate(sums)

    attended = with_layout_constraint(
        attend(projected, token_positions(z, y), head_size), Layout(major_to_minor=(0, 1))
    )
    across = send(attended, x=1)
    out_block, across = lax.optimization_barrier(
        (jnp.concatenate([near_block, near_crossed]), across)
    )

    def of_core(rows, place):
        by_core = rows.reshape(32, 2, 8, head_size)
        return jnp.where(place == 0, by_core[:, 0], by_core[:, 1])

    given_heads = send(
        jnp.concatenate([of_core(attended, 1 - core), of_core(across, 1 - core)], axis=2),
        core=1,
    )
    heads = jnp.concatenate(
        [of_core(attended, core), of_core(across, core), given_heads], axis=2
    )

    def turns(blocks):
        middle = jnp.where(core == 0, blocks[2], blocks[1])
        kept = jnp.where(core == 0, blocks[1], blocks[2])
        return [middle, blocks[3]], [blocks[0], kept]

    heads = heads.reshape(4, 2, 32, 4 * head_size)

    def out_rows_of(blocks):
        return jnp.dot(
            jnp.concatenate(blocks), out_block, preferred_element_type=jnp.float32
        )

    first_sent, first_kept = turns(heads[:, 0])
    second_sent, second_kept = turns(heads[:, 1])
    edges = out_rows_of(first_sent + second_sent).astype(jnp.bfloat16)
    rests = lax.optimization_barrier(out_rows_of(first_kept + second_kept))
    size = edges.shape[0] // 2
    totals = halve_sums(
        (edges[:size], edges[size:]), (rests[:size], rests[size:]), ("z", "y"), 1
    )
    middle = size // 2
    totals = halve_sums(
        [total[middle:] for total in totals], [total[:middle] for total in totals], ("z", "y"), 0
    )
    chunks = [turns(total.reshape(4, -1, half)) for total in totals]
    totals = halve_sums(
        [jnp.concatenate(sent) for sent, _ in chunks],
        [jnp.concatenate(kept) for _, kept in chunks],
        ("y", "z"),
        1,
    )
    first, second = lax.optimization_barrier(
        [total.astype(jnp.bfloat16).reshape(2, -1, half) for total in totals]
    )
    pairs_of = jnp.where(half_x == 0, first, second), jnp.where(half_x == 0, second, first)
    halves = []
    for crossed, rows in enumerate(pairs_of):
        own, near = (
            lax.ppermute(rows[k], AXES, owner_pairs(crossed, k)).astype(jnp.float32)
            for k in (0, 1)
        )
        halves.append((own + near).astype(jnp.bfloat16))
    straight, crossed = halves
    return jnp.where(
        half_x == 0,
        jnp.concatenate([straight, crossed], axis=1),
        jnp.concatenate([crossed, straight], axis=1),
    )[None]


def solution(mesh):
    placed = (
        P("pipe", "dp", None),
        P("pipe", None),
        P("pipe", None, "dp", None),
        P("pipe", "dp", None),
    )
    return jax.shard_map(
        shards, mesh=mesh, in_specs=placed, out_specs=P("pipe", "dp", None), check_vma=False
    )
```

```python
import math

import jax
import jax.numpy as jnp
import numpy as np
from jax import lax
from jax.experimental import pallas as pl
from jax.experimental.layout import Layout, with_layout_constraint
from jax.experimental.pallas import tpu as pltpu
from jax.sharding import PartitionSpec as P

RING = 4
AXES = ("pipe", "dp")


def split_place(index):
    core = index % 2
    y = index // 2 % 4
    half_x = index // 8 % 2
    z = index // 16 % 4
    pipe = index // 64
    return pipe, z, half_x, y, core


def role_of(z, y, core):
    return (core + z + y) % 2


def join_place(pipe, z, half_x, y, core):
    return (((pipe * 4 + z) * 2 + half_x) * 4 + y) * 2 + core


def send(value, pipe=0, z=0, x=0, y=0, core=0):
    pairs = []
    for source in range(128):
        p0, z0, x0, y0, c0 = split_place(source)
        target = join_place(p0 ^ pipe, (z0 + z) % 4, x0 ^ x, (y0 + y) % 4, c0 ^ core)
        pairs.append((source, target))
    return lax.ppermute(value, AXES, pairs)


def normalize_rows(role_ref, rows_ref, gain_ref, kept_ref, given_ref):
    values = rows_ref[...].astype(jnp.float32)
    centre = jnp.mean(values, axis=-1, keepdims=True)
    shifted = values - centre
    spread = jnp.mean(shifted * shifted, axis=-1, keepdims=True)
    normed = (shifted * lax.rsqrt(spread + 1e-05) * gain_ref[...]).astype(jnp.bfloat16)
    half = kept_ref.shape[1]

    @pl.when(role_ref[0] == 0)
    def _():
        kept_ref[...] = normed[:, :half]
        given_ref[...] = normed[:, half:]

    @pl.when(role_ref[0] != 0)
    def _():
        kept_ref[...] = normed[:, half:]
        given_ref[...] = normed[:, :half]


def normalize(section_rows, gain_vector, role):
    count, width = section_rows.shape
    part = pltpu.VMEM((count, width // 2), jnp.bfloat16)
    whole = pl.BlockSpec(memory_space=pltpu.VMEM)
    return pl.pallas_call(
        normalize_rows,
        out_shape=(part, part),
        in_specs=[pl.BlockSpec(memory_space=pltpu.SMEM), whole, whole],
        out_specs=(whole, whole),
    )(jnp.reshape(role, (1,)), section_rows, gain_vector)


def swap_pairs(axis, turn):
    pairs = []
    for source in range(128):
        pipe, z, half_x, y, core = split_place(source)
        flip = (1, 3)[turn ^ role_of(z, y, core)]
        if axis == "z":
            z ^= flip
        else:
            y ^= flip
        pairs.append((source, join_place(pipe, z, half_x, y, 1 - core)))
    return pairs


def swap_both(first, first_axis, second, second_axis, turn):
    return (
        lax.ppermute(first, AXES, swap_pairs(first_axis, turn)),
        lax.ppermute(second, AXES, swap_pairs(second_axis, turn)),
    )


def near_rows(own, one, two, role):
    size = own.shape[0]
    return jnp.concatenate(
        [
            own,
            jnp.where(role == 0, one, two[:size]),
            jnp.where(role == 0, two[:size], one),
            two[size:],
        ]
    )


def halve_sums(fars, nears, axes, turn):
    fars = lax.optimization_barrier([far.astype(jnp.bfloat16) for far in fars])
    got = lax.optimization_barrier(swap_both(fars[0], axes[0], fars[1], axes[1], turn))
    return [near + part.astype(jnp.float32) for near, part in zip(nears, got)]


def owner_pairs(crossed, near):
    pairs = []
    for source in range(128):
        pipe, z, half_x, y, core = split_place(source)
        half_x ^= crossed
        flip = (1, 3)[role_of(z, y, core)] if near else 0
        if half_x:
            z ^= flip
        else:
            y ^= flip
        pairs.append((source, join_place(1 - pipe, z, half_x, y, core ^ near)))
    return pairs


def token_positions(z, y):
    places = np.asarray([0, 1, 3, 2], np.int32)
    far = np.repeat(places, 128)
    side = np.tile(np.repeat(np.asarray([0, 1], np.int32), 64), 4)
    near = np.tile(np.repeat(places, 16), 8)
    low = np.tile(np.arange(16, dtype=np.int32), 32)
    dz = np.where(side == 0, far, near)
    dy = np.where(side == 0, near, far)
    return (((z ^ dz) * 2 + side) * 4 + (y ^ dy)) * 16 + low


def attend(projected, position, head_size):
    queries = projected[:, :head_size]
    keys_part = projected[:, head_size : 2 * head_size]
    values_part = projected[:, 2 * head_size :].astype(jnp.bfloat16)
    scores = jnp.einsum(
        "qd,kd->qk", queries, keys_part, precision=lax.Precision.HIGHEST
    ) / math.sqrt(head_size)
    causal = position[:, None] >= position[None, :]
    scores = jnp.where(causal, scores, -1e30)
    largest = jnp.max(scores, axis=-1, keepdims=True)
    weights = jnp.where(causal, jnp.exp(scores - largest), 0.0)
    totals = jnp.sum(weights, axis=-1, keepdims=True)
    probabilities = (weights / totals).astype(jnp.bfloat16)
    return jnp.dot(probabilities, values_part, preferred_element_type=jnp.float32).astype(
        jnp.bfloat16
    )


def shards(segment_input, norm_gain, head_weights, output_weights):
    head_size = output_weights.shape[1]
    width = segment_input.shape[2]
    half, quarter = width // 2, width // 4
    _, z, half_x, y, core = split_place(lax.axis_index("dp"))
    role = role_of(z, y, core)

    kept, given = normalize(segment_input[0], norm_gain, role)
    given = send(given, core=1)
    block = jnp.where(
        core == 0, jnp.concatenate([kept, given]), jnp.concatenate([given, kept])
    )
    head_block, block = lax.optimization_barrier((head_weights[0, :, 0, :], block))
    other = send(block, x=1)
    their_weights = lax.dynamic_slice_in_dim(head_block, (1 - role) * half, half, 0)
    swapped_weights = send(their_weights, core=1)
    first = jnp.where(half_x == 0, block, other)
    second = jnp.where(half_x == 0, other, block)
    own_weights = lax.dynamic_slice_in_dim(head_block, role * half, half, 0)

    one = swap_both(first, "y", second, "z", 0)
    two = swap_both(
        jnp.concatenate([first, one[0]]), "y", jnp.concatenate([second, one[1]]), "z", 1
    )
    first_own = near_rows(first, one[0], two[0], role)
    second_own = near_rows(second, one[1], two[1], role)

    out_rows, _ = lax.optimization_barrier((output_weights[0], block))
    out_kept = lax.dynamic_slice_in_dim(out_rows, half_x * half, half, 1)
    out_given = lax.dynamic_slice_in_dim(out_rows, (1 - half_x) * half, half, 1)
    out_given, _ = lax.optimization_barrier((out_given, one))
    out_across = send(out_given, x=1)

    def project(first_rows, second_rows):
        rows = jnp.concatenate([first_rows, second_rows])
        mine = jnp.dot(rows, own_weights, preferred_element_type=jnp.float32)
        theirs = jnp.dot(rows, swapped_weights, preferred_element_type=jnp.float32)
        return mine, theirs

    first_own, second_own, swapped_weights = lax.optimization_barrier(
        (first_own, second_own, swapped_weights)
    )
    turn_one = swap_both(first_own, "z", second_own, "y", 0)
    turn_two = swap_both(first_own, "z", second_own, "y", 1)
    here = [project(first_own, second_own)]
    turn_one, turn_two, here = lax.optimization_barrier((turn_one, turn_two, here))
    last = swap_both(turn_one[0], "z", turn_one[1], "y", 1)
    here.append(project(*turn_one))
    here.append(project(*turn_two))
    out_across, _ = lax.optimization_barrier((out_across, here))
    near_block = jnp.concatenate([out_kept, out_across])
    near_crossed = send(near_block, core=1)
    sums = [
        mine + send(theirs, core=1)
        for mine, theirs in (
            here[0],
            [jnp.where(role == 0, a, b) for a, b in zip(here[1], here[2])],
            [jnp.where(role == 0, b, a) for a, b in zip(here[1], here[2])],
        )
    ]
    last, sums = lax.optimization_barrier((last, sums))
    mine, theirs = project(*last)
    sums.append(lax.optimization_barrier(mine) + send(theirs, core=1))
    projected = jnp.concatenate(sums)

    attended = with_layout_constraint(
        attend(projected, token_positions(z, y), head_size), Layout(major_to_minor=(0, 1))
    )
    across = send(attended, x=1)
    out_block, across = lax.optimization_barrier(
        (jnp.concatenate([near_block, near_crossed]), across)
    )

    odd = np.asarray([0, 1, 1, 0])
    odd = (odd[:, None, None] ^ odd[None, None, :]) ^ np.zeros((1, 2, 1), np.int64)
    odd = odd.astype(np.int32).reshape(32, 1, 1)

    def of_core(rows, place):
        by_core = rows.reshape(32, 2, 8, head_size)
        return jnp.where((odd ^ place) == 0, by_core[:, 0], by_core[:, 1])

    given_heads = send(
        jnp.concatenate([of_core(attended, 1 - core), of_core(across, 1 - core)], axis=2),
        core=1,
    )
    heads = jnp.concatenate(
        [of_core(attended, core), of_core(across, core), given_heads], axis=2
    )

    def turns(blocks):
        middle = jnp.where(role == 0, blocks[2], blocks[1])
        kept = jnp.where(role == 0, blocks[1], blocks[2])
        return [middle, blocks[3]], [blocks[0], kept]

    heads = heads.reshape(4, 2, 32, 4 * head_size)

    def out_rows_of(blocks):
        return jnp.dot(
            jnp.concatenate(blocks), out_block, preferred_element_type=jnp.float32
        )

    first_sent, first_kept = turns(heads[:, 0])
    second_sent, second_kept = turns(heads[:, 1])
    edges = out_rows_of(first_sent + second_sent).astype(jnp.bfloat16)
    rests = lax.optimization_barrier(out_rows_of(first_kept + second_kept))
    size = edges.shape[0] // 2
    totals = halve_sums(
        (edges[:size], edges[size:]), (rests[:size], rests[size:]), ("z", "y"), 1
    )
    middle = size // 2
    totals = halve_sums(
        [total[middle:] for total in totals], [total[:middle] for total in totals], ("z", "y"), 0
    )
    chunks = [turns(total.reshape(4, -1, half)) for total in totals]
    totals = halve_sums(
        [jnp.concatenate(sent) for sent, _ in chunks],
        [jnp.concatenate(kept) for _, kept in chunks],
        ("y", "z"),
        1,
    )
    first, second = lax.optimization_barrier(
        [total.astype(jnp.bfloat16).reshape(2, -1, half) for total in totals]
    )
    pairs_of = jnp.where(half_x == 0, first, second), jnp.where(half_x == 0, second, first)
    halves = []
    for crossed, rows in enumerate(pairs_of):
        own, near = (
            lax.ppermute(rows[k], AXES, owner_pairs(crossed, k)).astype(jnp.float32)
            for k in (0, 1)
        )
        halves.append((own + near).astype(jnp.bfloat16))
    straight, crossed = halves
    return jnp.where(
        half_x == 0,
        jnp.concatenate([straight, crossed], axis=1),
        jnp.concatenate([crossed, straight], axis=1),
    )[None]


def solution(mesh):
    placed = (
        P("pipe", "dp", None),
        P("pipe", None),
        P("pipe", None, "dp", None),
        P("pipe", "dp", None),
    )
    return jax.shard_map(
        shards, mesh=mesh, in_specs=placed, out_specs=P("pipe", "dp", None), check_vma=False
    )
```

```python
import math

import jax
import jax.numpy as jnp
import numpy as np
from jax import lax
from jax.experimental import pallas as pl
from jax.experimental.layout import Layout, with_layout_constraint
from jax.experimental.pallas import tpu as pltpu
from jax.sharding import PartitionSpec as P

RING = 4
AXES = ("pipe", "dp")


def split_place(index):
    core = index % 2
    y = index // 2 % 4
    half_x = index // 8 % 2
    z = index // 16 % 4
    pipe = index // 64
    return pipe, z, half_x, y, core


def role_of(z, y, core):
    return (core + z + y) % 2


def join_place(pipe, z, half_x, y, core):
    return (((pipe * 4 + z) * 2 + half_x) * 4 + y) * 2 + core


def send(value, pipe=0, z=0, x=0, y=0, core=0):
    pairs = []
    for source in range(128):
        p0, z0, x0, y0, c0 = split_place(source)
        target = join_place(p0 ^ pipe, (z0 + z) % 4, x0 ^ x, (y0 + y) % 4, c0 ^ core)
        pairs.append((source, target))
    return lax.ppermute(value, AXES, pairs)


def normalize_rows(role_ref, rows_ref, gain_ref, kept_ref, given_ref):
    values = rows_ref[...].astype(jnp.float32)
    centre = jnp.mean(values, axis=-1, keepdims=True)
    shifted = values - centre
    spread = jnp.mean(shifted * shifted, axis=-1, keepdims=True)
    normed = (shifted * lax.rsqrt(spread + 1e-05) * gain_ref[...]).astype(jnp.bfloat16)
    half = kept_ref.shape[1]

    @pl.when(role_ref[0] == 0)
    def _():
        kept_ref[...] = normed[:, :half]
        given_ref[...] = normed[:, half:]

    @pl.when(role_ref[0] != 0)
    def _():
        kept_ref[...] = normed[:, half:]
        given_ref[...] = normed[:, :half]


def normalize(section_rows, gain_vector, role):
    count, width = section_rows.shape
    part = pltpu.VMEM((count, width // 2), jnp.bfloat16)
    whole = pl.BlockSpec(memory_space=pltpu.VMEM)
    return pl.pallas_call(
        normalize_rows,
        out_shape=(part, part),
        in_specs=[pl.BlockSpec(memory_space=pltpu.SMEM), whole, whole],
        out_specs=(whole, whole),
    )(jnp.reshape(role, (1,)), section_rows, gain_vector)


def swap_pairs(axis, turn):
    pairs = []
    for source in range(128):
        pipe, z, half_x, y, core = split_place(source)
        flip = (1, 3)[turn ^ role_of(z, y, core)]
        if axis == "z":
            z ^= flip
        else:
            y ^= flip
        pairs.append((source, join_place(pipe, z, half_x, y, 1 - core)))
    return pairs


def swap_both(first, first_axis, second, second_axis, turn):
    return (
        lax.ppermute(first, AXES, swap_pairs(first_axis, turn)),
        lax.ppermute(second, AXES, swap_pairs(second_axis, turn)),
    )


def near_rows(own, one, two, role):
    size = own.shape[0]
    return jnp.concatenate(
        [
            own,
            jnp.where(role == 0, one, two[:size]),
            jnp.where(role == 0, two[:size], one),
            two[size:],
        ]
    )


def halve_sums(fars, nears, axes, turn):
    fars = lax.optimization_barrier([far.astype(jnp.bfloat16) for far in fars])
    got = lax.optimization_barrier(swap_both(fars[0], axes[0], fars[1], axes[1], turn))
    return [near + part.astype(jnp.float32) for near, part in zip(nears, got)]


def owner_pairs(crossed, near):
    pairs = []
    for source in range(128):
        pipe, z, half_x, y, core = split_place(source)
        half_x ^= crossed
        flip = (1, 3)[role_of(z, y, core)] if near else 0
        if half_x:
            z ^= flip
        else:
            y ^= flip
        pairs.append((source, join_place(1 - pipe, z, half_x, y, core ^ near)))
    return pairs


def token_positions(z, y):
    places = np.asarray([0, 1, 3, 2], np.int32)
    far = np.repeat(places, 128)
    side = np.tile(np.repeat(np.asarray([0, 1], np.int32), 64), 4)
    near = np.tile(np.repeat(places, 16), 8)
    low = np.tile(np.arange(16, dtype=np.int32), 32)
    dz = np.where(side == 0, far, near)
    dy = np.where(side == 0, near, far)
    return (((z ^ dz) * 2 + side) * 4 + (y ^ dy)) * 16 + low


def attend(projected, position, head_size):
    queries = projected[:, :head_size]
    keys_part = projected[:, head_size : 2 * head_size]
    values_part = projected[:, 2 * head_size :].astype(jnp.bfloat16)
    scores = jnp.einsum(
        "qd,kd->qk", queries, keys_part, precision=lax.Precision.HIGHEST
    ) / math.sqrt(head_size)
    causal = position[:, None] >= position[None, :]
    scores = jnp.where(causal, scores, -1e30)
    largest = jnp.max(scores, axis=-1, keepdims=True)
    weights = jnp.where(causal, jnp.exp(scores - largest), 0.0)
    totals = jnp.sum(weights, axis=-1, keepdims=True)
    probabilities = (weights / totals).astype(jnp.bfloat16)
    return jnp.dot(probabilities, values_part, preferred_element_type=jnp.float32).astype(
        jnp.bfloat16
    )


def shards(segment_input, norm_gain, head_weights, output_weights):
    head_size = output_weights.shape[1]
    width = segment_input.shape[2]
    half, quarter = width // 2, width // 4
    _, z, half_x, y, core = split_place(lax.axis_index("dp"))
    role = role_of(z, y, core)

    kept, given = normalize(segment_input[0], norm_gain, role)
    kept, given = lax.optimization_barrier((kept, given))
    across, across_other = send(kept, x=1), send(given, x=1, core=1)
    beside = send(given, core=1)

    def in_core_order(mine, others):
        return jnp.where(
            core == 0, jnp.concatenate([mine, others]), jnp.concatenate([others, mine])
        )

    head_block, beside = lax.optimization_barrier((head_weights[0, :, 0, :], beside))
    their_weights = lax.dynamic_slice_in_dim(head_block, (1 - role) * half, half, 0)
    across, _ = lax.optimization_barrier((across, their_weights))
    block, other = in_core_order(kept, beside), in_core_order(across, across_other)
    swapped_weights = send(their_weights, core=1)
    first = jnp.where(half_x == 0, block, other)
    second = jnp.where(half_x == 0, other, block)
    own_weights = lax.dynamic_slice_in_dim(head_block, role * half, half, 0)

    one = swap_both(first, "y", second, "z", 0)
    two = swap_both(
        jnp.concatenate([first, one[0]]), "y", jnp.concatenate([second, one[1]]), "z", 1
    )
    first_own = near_rows(first, one[0], two[0], role)
    second_own = near_rows(second, one[1], two[1], role)

    out_rows, _ = lax.optimization_barrier((output_weights[0], block))
    out_kept = lax.dynamic_slice_in_dim(out_rows, half_x * half, half, 1)
    out_given = lax.dynamic_slice_in_dim(out_rows, (1 - half_x) * half, half, 1)
    out_given, _ = lax.optimization_barrier((out_given, one))
    out_across = send(out_given, x=1)

    def project(first_rows, second_rows):
        rows = jnp.concatenate([first_rows, second_rows])
        mine = jnp.dot(rows, own_weights, preferred_element_type=jnp.float32)
        theirs = jnp.dot(rows, swapped_weights, preferred_element_type=jnp.float32)
        return mine, theirs

    first_own, second_own, swapped_weights = lax.optimization_barrier(
        (first_own, second_own, swapped_weights)
    )
    turn_one = swap_both(first_own, "z", second_own, "y", 0)
    turn_two = swap_both(first_own, "z", second_own, "y", 1)
    here = [project(first_own, second_own)]
    turn_one, turn_two, here = lax.optimization_barrier((turn_one, turn_two, here))
    last = swap_both(turn_one[0], "z", turn_one[1], "y", 1)
    here.append(project(*turn_one))
    here.append(project(*turn_two))
    out_across, _ = lax.optimization_barrier((out_across, here))
    near_block = jnp.concatenate([out_kept, out_across])
    near_crossed = send(near_block, core=1)
    sums = [
        mine + send(theirs, core=1)
        for mine, theirs in (
            here[0],
            [jnp.where(role == 0, a, b) for a, b in zip(here[1], here[2])],
            [jnp.where(role == 0, b, a) for a, b in zip(here[1], here[2])],
        )
    ]
    last, sums = lax.optimization_barrier((last, sums))
    mine, theirs = project(*last)
    sums.append(lax.optimization_barrier(mine) + send(theirs, core=1))
    projected = jnp.concatenate(sums)

    attended = with_layout_constraint(
        attend(projected, token_positions(z, y), head_size), Layout(major_to_minor=(0, 1))
    )
    across = send(attended, x=1)
    out_block, across = lax.optimization_barrier(
        (jnp.concatenate([near_block, near_crossed]), across)
    )

    odd = np.asarray([0, 1, 1, 0])
    odd = (odd[:, None, None] ^ odd[None, None, :]) ^ np.zeros((1, 2, 1), np.int64)
    odd = odd.astype(np.int32).reshape(32, 1, 1)

    def of_core(rows, place):
        by_core = rows.reshape(32, 2, 8, head_size)
        return jnp.where((odd ^ place) == 0, by_core[:, 0], by_core[:, 1])

    given_heads = send(
        jnp.concatenate([of_core(attended, 1 - core), of_core(across, 1 - core)], axis=2),
        core=1,
    )
    heads = jnp.concatenate(
        [of_core(attended, core), of_core(across, core), given_heads], axis=2
    )

    def turns(blocks):
        middle = jnp.where(role == 0, blocks[2], blocks[1])
        kept = jnp.where(role == 0, blocks[1], blocks[2])
        return [middle, blocks[3]], [blocks[0], kept]

    heads = heads.reshape(4, 2, 32, 4 * head_size)

    def out_rows_of(blocks):
        return jnp.dot(
            jnp.concatenate(blocks), out_block, preferred_element_type=jnp.float32
        )

    first_sent, first_kept = turns(heads[:, 0])
    second_sent, second_kept = turns(heads[:, 1])
    edges = out_rows_of(first_sent + second_sent).astype(jnp.bfloat16)
    rests = lax.optimization_barrier(out_rows_of(first_kept + second_kept))
    size = edges.shape[0] // 2
    totals = halve_sums(
        (edges[:size], edges[size:]), (rests[:size], rests[size:]), ("z", "y"), 1
    )
    middle = size // 2
    totals = halve_sums(
        [total[middle:] for total in totals], [total[:middle] for total in totals], ("z", "y"), 0
    )
    chunks = [turns(total.reshape(4, -1, half)) for total in totals]
    totals = halve_sums(
        [jnp.concatenate(sent) for sent, _ in chunks],
        [jnp.concatenate(kept) for _, kept in chunks],
        ("y", "z"),
        1,
    )
    first, second = lax.optimization_barrier(
        [total.astype(jnp.bfloat16).reshape(2, -1, half) for total in totals]
    )
    pairs_of = jnp.where(half_x == 0, first, second), jnp.where(half_x == 0, second, first)
    parts = {
        (crossed, near): lax.ppermute(
            pairs_of[crossed][near], AXES, owner_pairs(crossed, near)
        ).astype(jnp.float32)
        for near in (1, 0)
        for crossed in (1, 0)
    }
    straight, crossed = (
        (parts[k, 0] + parts[k, 1]).astype(jnp.bfloat16) for k in (0, 1)
    )
    return jnp.where(
        half_x == 0,
        jnp.concatenate([straight, crossed], axis=1),
        jnp.concatenate([crossed, straight], axis=1),
    )[None]


def solution(mesh):
    placed = (
        P("pipe", "dp", None),
        P("pipe", None),
        P("pipe", None, "dp", None),
        P("pipe", "dp", None),
    )
    return jax.shard_map(
        shards, mesh=mesh, in_specs=placed, out_specs=P("pipe", "dp", None), check_vma=False
    )
```

```python
import math

import jax
import jax.numpy as jnp
import numpy as np
from jax import lax
from jax.experimental import pallas as pl
from jax.experimental.layout import Layout, with_layout_constraint
from jax.experimental.pallas import tpu as pltpu
from jax.sharding import PartitionSpec as P

RING = 4
AXES = ("pipe", "dp")


def split_place(index):
    core = index % 2
    y = index // 2 % 4
    half_x = index // 8 % 2
    z = index // 16 % 4
    pipe = index // 64
    return pipe, z, half_x, y, core


def role_of(z, y, core):
    return (core + z + y) % 2


def join_place(pipe, z, half_x, y, core):
    return (((pipe * 4 + z) * 2 + half_x) * 4 + y) * 2 + core


def send(value, pipe=0, z=0, x=0, y=0, core=0):
    pairs = []
    for source in range(128):
        p0, z0, x0, y0, c0 = split_place(source)
        target = join_place(p0 ^ pipe, (z0 + z) % 4, x0 ^ x, (y0 + y) % 4, c0 ^ core)
        pairs.append((source, target))
    return lax.ppermute(value, AXES, pairs)


def normalize_rows(role_ref, rows_ref, gain_ref, kept_ref, given_ref):
    values = rows_ref[...].astype(jnp.float32)
    centre = jnp.mean(values, axis=-1, keepdims=True)
    shifted = values - centre
    spread = jnp.mean(shifted * shifted, axis=-1, keepdims=True)
    normed = (shifted * lax.rsqrt(spread + 1e-05) * gain_ref[...]).astype(jnp.bfloat16)
    half = kept_ref.shape[1]

    @pl.when(role_ref[0] == 0)
    def _():
        kept_ref[...] = normed[:, :half]
        given_ref[...] = normed[:, half:]

    @pl.when(role_ref[0] != 0)
    def _():
        kept_ref[...] = normed[:, half:]
        given_ref[...] = normed[:, :half]


def normalize(section_rows, gain_vector, role):
    count, width = section_rows.shape
    part = pltpu.VMEM((count, width // 2), jnp.bfloat16)
    whole = pl.BlockSpec(memory_space=pltpu.VMEM)
    return pl.pallas_call(
        normalize_rows,
        out_shape=(part, part),
        in_specs=[pl.BlockSpec(memory_space=pltpu.SMEM), whole, whole],
        out_specs=(whole, whole),
    )(jnp.reshape(role, (1,)), section_rows, gain_vector)


def swap_pairs(axis, turn):
    pairs = []
    for source in range(128):
        pipe, z, half_x, y, core = split_place(source)
        flip = (1, 3)[turn ^ role_of(z, y, core)]
        if axis == "z":
            z ^= flip
        else:
            y ^= flip
        pairs.append((source, join_place(pipe, z, half_x, y, 1 - core)))
    return pairs


def swap_both(first, first_axis, second, second_axis, turn):
    return (
        lax.ppermute(first, AXES, swap_pairs(first_axis, turn)),
        lax.ppermute(second, AXES, swap_pairs(second_axis, turn)),
    )


def near_rows(own, one, two, role):
    size = own.shape[0]
    return jnp.concatenate(
        [
            own,
            jnp.where(role == 0, one, two[:size]),
            jnp.where(role == 0, two[:size], one),
            two[size:],
        ]
    )


def halve_sums(fars, nears, axes, turn):
    fars = lax.optimization_barrier([far.astype(jnp.bfloat16) for far in fars])
    got = lax.optimization_barrier(swap_both(fars[0], axes[0], fars[1], axes[1], turn))
    return [near + part.astype(jnp.float32) for near, part in zip(nears, got)]


def owner_pairs(crossed, near):
    pairs = []
    for source in range(128):
        pipe, z, half_x, y, core = split_place(source)
        half_x ^= crossed
        flip = (1, 3)[role_of(z, y, core)] if near else 0
        if half_x:
            z ^= flip
        else:
            y ^= flip
        pairs.append((source, join_place(1 - pipe, z, half_x, y, core ^ near)))
    return pairs


def token_positions(z, y):
    places = np.asarray([0, 1, 3, 2], np.int32)
    far = np.repeat(places, 128)
    side = np.tile(np.repeat(np.asarray([0, 1], np.int32), 64), 4)
    near = np.tile(np.repeat(places, 16), 8)
    low = np.tile(np.arange(16, dtype=np.int32), 32)
    dz = np.where(side == 0, far, near)
    dy = np.where(side == 0, near, far)
    return (((z ^ dz) * 2 + side) * 4 + (y ^ dy)) * 16 + low


def attend(projected, position, head_size):
    queries = projected[:, :head_size]
    keys_part = projected[:, head_size : 2 * head_size]
    values_part = projected[:, 2 * head_size :].astype(jnp.bfloat16)
    scores = jnp.einsum(
        "qd,kd->qk", queries, keys_part, precision=lax.Precision.HIGHEST
    ) / math.sqrt(head_size)
    causal = position[:, None] >= position[None, :]
    scores = jnp.where(causal, scores, -1e30)
    largest = jnp.max(scores, axis=-1, keepdims=True)
    weights = jnp.where(causal, jnp.exp(scores - largest), 0.0)
    totals = jnp.sum(weights, axis=-1, keepdims=True)
    probabilities = (weights / totals).astype(jnp.bfloat16)
    return jnp.dot(probabilities, values_part, preferred_element_type=jnp.float32).astype(
        jnp.bfloat16
    )


def shards(segment_input, norm_gain, head_weights, output_weights):
    head_size = output_weights.shape[1]
    width = segment_input.shape[2]
    half, quarter = width // 2, width // 4
    _, z, half_x, y, core = split_place(lax.axis_index("dp"))
    role = role_of(z, y, core)

    kept, given = normalize(segment_input[0], norm_gain, role)
    kept, given = lax.optimization_barrier((kept, given))
    across, across_other = send(kept, x=1), send(given, x=1, core=1)
    beside = send(given, core=1)

    def in_core_order(mine, others):
        return jnp.where(
            core == 0, jnp.concatenate([mine, others]), jnp.concatenate([others, mine])
        )

    head_block, beside = lax.optimization_barrier((head_weights[0, :, 0, :], beside))
    their_weights = lax.dynamic_slice_in_dim(head_block, (1 - role) * half, half, 0)
    across, _ = lax.optimization_barrier((across, their_weights))
    block, other = in_core_order(kept, beside), in_core_order(across, across_other)
    swapped_weights = send(their_weights, core=1)
    first = jnp.where(half_x == 0, block, other)
    second = jnp.where(half_x == 0, other, block)
    own_weights = lax.dynamic_slice_in_dim(head_block, role * half, half, 0)

    one = swap_both(first, "y", second, "z", 0)
    two = swap_both(
        jnp.concatenate([first, one[0]]), "y", jnp.concatenate([second, one[1]]), "z", 1
    )
    first_own = near_rows(first, one[0], two[0], role)
    second_own = near_rows(second, one[1], two[1], role)

    out_rows, _ = lax.optimization_barrier((output_weights[0], first))
    out_kept = lax.dynamic_slice_in_dim(out_rows, half_x * half, half, 1)
    out_given = lax.dynamic_slice_in_dim(out_rows, (1 - half_x) * half, half, 1)
    out_given, _ = lax.optimization_barrier((out_given, one))
    out_across = send(out_given, x=1)

    def project(first_rows, second_rows):
        rows = jnp.concatenate([first_rows, second_rows])
        mine = jnp.dot(rows, own_weights, preferred_element_type=jnp.float32)
        theirs = jnp.dot(rows, swapped_weights, preferred_element_type=jnp.float32)
        return mine, theirs

    first_own, second_own, swapped_weights = lax.optimization_barrier(
        (first_own, second_own, swapped_weights)
    )
    turn_one = swap_both(first_own, "z", second_own, "y", 0)
    turn_two = swap_both(first_own, "z", second_own, "y", 1)
    here = [project(first_own, second_own)]
    turn_one, turn_two, here = lax.optimization_barrier((turn_one, turn_two, here))
    last = swap_both(turn_one[0], "z", turn_one[1], "y", 1)
    here.append(project(*turn_one))
    here.append(project(*turn_two))
    out_across, _ = lax.optimization_barrier((out_across, here))
    near_block = jnp.concatenate([out_kept, out_across])
    near_crossed = send(near_block, core=1)
    sums = [
        mine + send(theirs, core=1)
        for mine, theirs in (
            here[0],
            [jnp.where(role == 0, a, b) for a, b in zip(here[1], here[2])],
            [jnp.where(role == 0, b, a) for a, b in zip(here[1], here[2])],
        )
    ]
    last, sums = lax.optimization_barrier((last, sums))
    mine, theirs = project(*last)
    sums.append(lax.optimization_barrier(mine) + send(theirs, core=1))
    projected = jnp.concatenate(sums)

    attended = with_layout_constraint(
        attend(projected, token_positions(z, y), head_size), Layout(major_to_minor=(0, 1))
    )
    across = send(attended, x=1)
    out_block, across = lax.optimization_barrier(
        (jnp.concatenate([near_block, near_crossed]), across)
    )

    odd = np.asarray([0, 1, 1, 0])
    odd = (odd[:, None, None] ^ odd[None, None, :]) ^ np.zeros((1, 2, 1), np.int64)
    odd = odd.astype(np.int32).reshape(32, 1, 1)

    def of_core(rows, place):
        by_core = rows.reshape(32, 2, 8, head_size)
        return jnp.where((odd ^ place) == 0, by_core[:, 0], by_core[:, 1])

    given_heads = send(
        jnp.concatenate([of_core(attended, 1 - core), of_core(across, 1 - core)], axis=2),
        core=1,
    )
    heads = jnp.concatenate(
        [of_core(attended, core), of_core(across, core), given_heads], axis=2
    )

    def turns(blocks):
        middle = jnp.where(role == 0, blocks[2], blocks[1])
        kept = jnp.where(role == 0, blocks[1], blocks[2])
        return [middle, blocks[3]], [blocks[0], kept]

    heads = heads.reshape(4, 2, 32, 4 * head_size)

    def out_rows_of(blocks):
        return jnp.dot(
            jnp.concatenate(blocks), out_block, preferred_element_type=jnp.float32
        )

    first_sent, first_kept = turns(heads[:, 0])
    second_sent, second_kept = turns(heads[:, 1])
    edges = out_rows_of(first_sent + second_sent).astype(jnp.bfloat16)
    rests = lax.optimization_barrier(out_rows_of(first_kept + second_kept))
    size = edges.shape[0] // 2
    totals = halve_sums(
        (edges[:size], edges[size:]), (rests[:size], rests[size:]), ("z", "y"), 1
    )
    middle = size // 2
    totals = halve_sums(
        [total[middle:] for total in totals], [total[:middle] for total in totals], ("z", "y"), 0
    )
    chunks = [turns(total.reshape(4, -1, half)) for total in totals]
    totals = halve_sums(
        [jnp.concatenate(sent) for sent, _ in chunks],
        [jnp.concatenate(kept) for _, kept in chunks],
        ("y", "z"),
        1,
    )
    first, second = lax.optimization_barrier(
        [total.astype(jnp.bfloat16).reshape(2, -1, half) for total in totals]
    )
    pairs_of = jnp.where(half_x == 0, first, second), jnp.where(half_x == 0, second, first)
    parts = {
        (crossed, near): lax.ppermute(
            pairs_of[crossed][near], AXES, owner_pairs(crossed, near)
        ).astype(jnp.float32)
        for near in (1, 0)
        for crossed in (1, 0)
    }
    straight, crossed = (
        (parts[k, 0] + parts[k, 1]).astype(jnp.bfloat16) for k in (0, 1)
    )
    return jnp.where(
        half_x == 0,
        jnp.concatenate([straight, crossed], axis=1),
        jnp.concatenate([crossed, straight], axis=1),
    )[None]


def solution(mesh):
    placed = (
        P("pipe", "dp", None),
        P("pipe", None),
        P("pipe", None, "dp", None),
        P("pipe", "dp", None),
    )
    return jax.shard_map(
        shards, mesh=mesh, in_specs=placed, out_specs=P("pipe", "dp", None), check_vma=False
    )
```
